32 devices in a mesh: dp: 4 (over x, core), ep: 8 (over z, y).
Axes of the slice: x: 2, y: 2, z: 4, core: 2. Of those that a mesh axis runs over, the one named last changes fastest.
Arguments:
- tokens: bfloat16 [4, 4096, 1280], P('dp', 'ep'), may hold values from -6 to 6
- cotangent: bfloat16 [4, 4096, 1280], P('dp', 'ep'), may hold values from -6 to 6
- expert_ids: int32 [4, 4096, 7], P('dp', 'ep'), may hold values from 0 to 15, all different within a row; in each aligned block of 512 rows (0 to 511, 512 to 1023, ..., all dimensions but the last counted through in order) at most 320 rows name the same one
- keep: int32 [4, 4096, 7], P('dp', 'ep'), may hold values 0 or 1
- gates: float32 [4, 4096, 7], P('dp', 'ep'), may hold values from 0.25 to 0.75
- norm1_gain: bfloat16 [1280], P(('dp', 'ep')), may hold values from 0.5 to 1.5
- norm2_gain: bfloat16 [1280], P(('dp', 'ep')), may hold values from 0.5 to 1.5
- w_query: bfloat16 [1280, 1280], P(('dp', 'ep')), may hold values from -0.25 to 0.25
- w_key: bfloat16 [1280, 1280], P(('dp', 'ep')), may hold values from -0.25 to 0.25
- w_value: bfloat16 [1280, 1280], P(('dp', 'ep')), may hold values from -0.15625 to 0.15625
- w_out: bfloat16 [1280, 1280], P(('dp', 'ep')), may hold values from -0.625 to 0.625
- shared_gate: bfloat16 [1280, 896], P(('dp', 'ep')), may hold values from -0.15625 to 0.15625
- shared_up: bfloat16 [1280, 896], P(('dp', 'ep')), may hold values from -0.15625 to 0.15625
- shared_down: bfloat16 [896, 1280], P(None, ('dp', 'ep')), may hold values from -0.375 to 0.375
- expert_gate: bfloat16 [16, 1280, 896], P('ep'), may hold values from -0.15625 to 0.15625
- expert_up: bfloat16 [16, 1280, 896], P('ep'), may hold values from -0.15625 to 0.15625
- expert_down: bfloat16 [16, 896, 1280], P('ep'), may hold values from -0.375 to 0.375
Outputs:
- output: bfloat16 [4, 4096, 1280], P('dp', 'ep')
- grad_input: float32 [4, 4096, 1280], P('dp', 'ep')
- grad_norm1_gain: float32 [1280], P(('dp', 'ep'))
- grad_norm2_gain: float32 [1280], P(('dp', 'ep'))
- grad_w_query: float32 [1280, 1280], P(('dp', 'ep'))
- grad_w_key: float32 [1280, 1280], P(('dp', 'ep'))
- grad_w_value: float32 [1280, 1280], P(('dp', 'ep'))
- grad_w_out: float32 [1280, 1280], P(('dp', 'ep'))
- grad_shared_gate: float32 [1280, 896], P(('dp', 'ep'))
- grad_shared_up: float32 [1280, 896], P(('dp', 'ep'))
- grad_shared_down: float32 [896, 1280], P(None, ('dp', 'ep'))
- grad_expert_gate: float32 [16, 1280, 896], P('ep', 'dp')
- grad_expert_up: float32 [16, 1280, 896], P('ep', 'dp')
- grad_expert_down: float32 [16, 896, 1280], P('ep', None, 'dp')
The draws below stay inside these ranges and needn't reach their ends.
Inputs may be any that keep to these rules, and one draw needn't show every extreme that they name: `expert_ids`: each token names 7 different experts; among the tokens of one device (aligned blocks of 512 tokens of a sequence) no expert is named by more than 320.
All inputs are finite; a program needn't handle non-finite values. No bound on the sum of `keep` on one device may be relied on, other than what follows from the above.
Results may differ from the reference program's by a relative error of at most 0.025.
Values may be sent and summed in bfloat16 or wider, within the bound.
No kernel may reach another device: no remote copies, remote signals or barrier semaphores. Data moves between devices by JAX's collectives and lax.ppermute only.
A program may use at most 320 MiB of HBM per device.

```python
import math
import jax
import jax.numpy as jnp
import numpy as np
from jax import lax

D = 1280
HEADS = 10
HEAD = 128
FF = 896
TOP = 7
LENGTH = 4096
EXPERTS = 16
GROUPS = 4
TOK = 512
CAP = 320


def touch_ends(result, key, low, high):
    longest = result.shape.index(max(result.shape))
    spots = []
    for shift in (0, 1):
        where = [jax.random.randint(jax.random.fold_in(key, axis), (), 0, length) for axis, length in enumerate(result.shape)]
        where[longest] = (where[longest] + shift) % result.shape[longest]
        spots.append(tuple(where))
    return result.at[spots[0]].set(low).at[spots[1]].set(high)


def levels(own_key, shape, split, least, largest):
    def one(axis_at, blocks):
        draws = jax.random.uniform(jax.random.fold_in(jax.random.fold_in(own_key, 6), axis_at), (blocks,), jnp.float32, least / len(split), largest / len(split))
        return jnp.repeat(jnp.exp(draws), shape[axis_at] // blocks).reshape((-1,) + (1,) * (len(shape) - axis_at - 1))

    loudness = one(*split[0])
    for cut in split[1:]:
        loudness = loudness * one(*cut)
    return loudness


def deal_out(own_key, own, number, rows, count, top, limit, lean):
    ranking = jax.random.permutation(own_key, count)
    packed, ordinary = portions_of(count, rows * top, limit, lean, True), portions_of(count, rows * top, limit, lean, False)
    places = jnp.arange(count)

    def named(tallies, offset_by):
        used = int((tallies > 0).sum())
        fixed = max(1, used // 4)
        shifted = fixed + (places - fixed + offset_by * (used - fixed)) % max(1, count - fixed)
        return jnp.zeros((count,), jnp.int32).at[ranking[jnp.where(places < fixed, places, shifted)]].set(jnp.asarray(tallies, jnp.int32))

    tallies = jnp.where(number % 4 == 0, named(packed, number // 4), named(ordinary, number - number // 4 - 1))
    mixed = jax.random.permutation(jax.random.fold_in(own, 3), count)
    source_of, sink = mixed[0:count // 2 * 2:2], mixed[1:count // 2 * 2:2]
    room = jnp.minimum(tallies[source_of] - 1, limit - tallies[sink]) // 2
    room = jnp.where((source_of == ranking[0]) | (sink == ranking[0]) | (tallies[sink] == 0), 0, jnp.maximum(room, 0))
    shifted = jax.random.randint(jax.random.fold_in(own, 4), (count // 2,), 0, 1 << 20) % (room + 1)
    tallies = tallies.at[source_of].add(-shifted).at[sink].add(shifted)
    labels = jnp.searchsorted(jnp.cumsum(tallies), jnp.arange(rows * top), side="right").astype(jnp.int32)
    listing = labels.reshape(top, rows).T
    listing = listing[jax.random.permutation(jax.random.fold_in(own, 1), rows)]
    offset_by = jax.random.randint(jax.random.fold_in(own, 2), (rows, 1), 0, top)
    return jnp.take_along_axis(listing, (jnp.arange(top)[None, :] + offset_by) % top, axis=1)


def portions_of(count, total, reach, slope, full):
    loads = [(1 << 20) // math.isqrt(standing ** slope) + 1 for standing in range(1, count + 1)]
    largest = reach if full else min(reach, max(-(-total // count), total * loads[0] // sum(loads)))
    least = 1 if total - largest >= count - 1 else 0
    counts, surplus = [largest] + [least] * (count - 1), total - largest - least * (count - 1)
    while surplus > 0:
        free = [i for i in range(1, count) if counts[i] < largest] or [i for i in range(1, count) if counts[i] < reach]
        pool, left = sum([loads[i] for i in free]), surplus
        for i in free:
            extra = min(reach - counts[i], max(1, left * loads[i] // pool), surplus)
            counts[i] = counts[i] + extra
            surplus = surplus - extra
    return np.array(counts)


def gaussian(own_key, shape, width, reach, cuts=(), kind=jnp.bfloat16):
    level = levels(own_key, shape, cuts, -0.22, 0.18) if cuts else 1.0
    values = jax.random.normal(own_key, shape, jnp.float32) * width * level
    return jnp.minimum(jnp.maximum(values, -reach), reach).astype(kind)


def setup_inputs(seed: int = 0) -> dict:
    streams_of = jax.random.split(jax.random.key(seed), 18)
    tokens = gaussian(streams_of[0], (GROUPS, LENGTH, D), 1.0, 6.0, ((0, 4), (1, 8)))
    cotangent = gaussian(streams_of[1], (GROUPS, LENGTH, D), 1.0, 6.0, ((0, 4), (1, 8)))
    expert_ids_keys = jax.random.split(jax.random.fold_in(streams_of[2], 1), GROUPS * LENGTH // TOK)
    expert_ids_turns = jax.random.permutation(jax.random.fold_in(streams_of[2], 3), GROUPS * LENGTH // TOK)
    expert_ids = jax.vmap(lambda own, number: deal_out(jax.random.fold_in(streams_of[2], 2), own, number, TOK, EXPERTS, TOP, CAP, 1))(expert_ids_keys, expert_ids_turns).reshape((GROUPS, LENGTH, TOP))
    keep = touch_ends((jax.random.randint(streams_of[3], (GROUPS, LENGTH, TOP), 0, 16) < 15).astype(jnp.int32), jax.random.fold_in(streams_of[3], 1), 0, 1)
    gates = jnp.clip(0.25 + 0.5 * jax.random.uniform(streams_of[4], (GROUPS, LENGTH, TOP), jnp.float32) ** levels(streams_of[4], (GROUPS, LENGTH, TOP), ((0, 4), (1, 8)), -0.2, 0.2), 0.25, 0.75)
    norm1_gain = jnp.clip(1.0 + 0.1 * jax.random.normal(streams_of[5], (D,), jnp.float32), 0.5, 1.5).astype(jnp.bfloat16)
    norm2_gain = jnp.clip(1.0 + 0.1 * jax.random.normal(streams_of[6], (D,), jnp.float32), 0.5, 1.5).astype(jnp.bfloat16)
    w_query = gaussian(streams_of[7], (D, D), (D // 2) ** -0.5, 0.25, ((0, 32),))
    w_key = gaussian(streams_of[8], (D, D), (D // 2) ** -0.5, 0.25, ((0, 32),))
    w_value = gaussian(streams_of[9], (D, D), D ** -0.5, 0.15625, ((0, 32),))
    w_out = gaussian(streams_of[10], (D, D), (D // 16) ** -0.5, 0.625, ((0, 32),))
    shared_gate = gaussian(streams_of[11], (D, FF), D ** -0.5, 0.15625, ((0, 32),))
    shared_up = gaussian(streams_of[12], (D, FF), D ** -0.5, 0.15625, ((0, 32),))
    shared_down = gaussian(streams_of[13], (FF, D), (FF // 4) ** -0.5, 0.375, ((1, 32),))
    expert_gate = gaussian(streams_of[14], (EXPERTS, D, FF), D ** -0.5, 0.15625, ((0, 8),))
    expert_up = gaussian(streams_of[15], (EXPERTS, D, FF), D ** -0.5, 0.15625, ((0, 8),))
    expert_down = gaussian(streams_of[16], (EXPERTS, FF, D), (FF // 4) ** -0.5, 0.375, ((0, 8),))
    return dict(tokens=tokens, cotangent=cotangent, expert_ids=expert_ids, keep=keep, gates=gates, norm1_gain=norm1_gain, norm2_gain=norm2_gain, w_query=w_query, w_key=w_key, w_value=w_value, w_out=w_out, shared_gate=shared_gate, shared_up=shared_up, shared_down=shared_down, expert_gate=expert_gate, expert_up=expert_up, expert_down=expert_down)


@jax.custom_vjp
def low(v):
    return lax.optimization_barrier(v.astype(jnp.bfloat16)).astype(jnp.float32)

@jax.custom_vjp
def low_back(v):
    return v

def low_keep(v):
    return (low(v), None)

def low_pass(kept, grad):
    return (grad,)

def back_keep(v):
    return (v, None)

def back_low(kept, grad):
    return (low(grad),)
low.defvjp(low_keep, low_pass)
low_back.defvjp(back_keep, back_low)
epsilon = 1e-06
negative = -1e+30
highest = lax.Precision.HIGHEST

def angles(first, length, head_dim):
    half = head_dim // 2
    freqs = jnp.exp(jnp.arange(half, dtype=jnp.float32) * (-2.0 * math.log(10000.0) / head_dim))
    places = (first + jnp.arange(length, dtype=jnp.int32)).astype(jnp.float32)
    turned = places[:, None] * freqs[None, :]
    return (jnp.cos(turned)[:, None, :], jnp.sin(turned)[:, None, :])

def rotate(values, cosine, sine):
    half = values.shape[-1] // 2
    first_half = values[..., :half]
    second_half = values[..., half:]
    return jnp.concatenate([first_half * cosine - second_half * sine, second_half * cosine + first_half * sine], axis=-1)

def normalize(values, gain):
    inverse = lax.rsqrt(lax.optimization_barrier(jnp.mean(values * values, axis=-1, keepdims=True)) + epsilon)
    return values * inverse * gain

def attend_block(block_inputs, keys, values):
    block_queries, first = block_inputs
    span = block_queries.shape[0]
    scores = jnp.einsum('qhd,khd->hqk', block_queries, keys, precision=highest) * (1.0 / math.sqrt(HEAD))
    query_places = first + jnp.arange(span, dtype=jnp.int32)
    key_places = jnp.arange(keys.shape[0], dtype=jnp.int32)
    visible = query_places[:, None] >= key_places[None, :]
    scores = low_back(jnp.where(visible[None], scores, negative))
    probs = jax.nn.softmax(scores, axis=-1)
    return jnp.einsum('hqk,khd->qhd', low(probs), values, precision=highest)

def layer(tokens, gain_one, gain_two, w_query, w_key, w_value, w_out, shared_gate, shared_up, shared_down, expert_gate, expert_up, expert_down, route_weight):
    length = tokens.shape[0]
    cosine, sine = angles(0, length, HEAD)
    hidden_one = low(normalize(tokens, gain_one))
    query_pre = low_back(jnp.dot(hidden_one, w_query, precision=highest)).reshape(length, HEADS, HEAD)
    key_pre = low_back(jnp.dot(hidden_one, w_key, precision=highest)).reshape(length, HEADS, HEAD)
    queries = low(rotate(query_pre, cosine, sine))
    keys = low(rotate(key_pre, cosine, sine))
    values = low(low_back(jnp.dot(hidden_one, w_value, precision=highest))).reshape(length, HEADS, HEAD)
    span = min(512, length)
    blocks = queries.reshape(length // span, span, HEADS, HEAD)
    firsts = jnp.arange(length // span, dtype=jnp.int32) * span
    attend = jax.checkpoint(attend_block)
    attended = lax.map(lambda inputs: attend(inputs, keys, values), (blocks, firsts)).reshape(length, HEADS * HEAD)
    attended = low_back(low(attended))
    branch = low_back(jnp.dot(attended, w_out, precision=highest))
    middle = tokens + branch
    hidden_two = low(normalize(middle, gain_two))
    shared_gate_pre = low_back(jnp.dot(hidden_two, shared_gate, precision=highest))
    shared_up_pre = low_back(jnp.dot(hidden_two, shared_up, precision=highest))
    shared_act = low(jax.nn.silu(shared_gate_pre) * shared_up_pre)
    shared_branch = low_back(jnp.dot(shared_act, shared_down, precision=highest))

    def one_expert(running, inputs):
        gate_weight, up_weight, down_weight, column = inputs
        copies = low_back(hidden_two)
        gate_pre = low_back(jnp.dot(copies, gate_weight, precision=highest))
        up_pre = low_back(jnp.dot(copies, up_weight, precision=highest))
        activated = low(jax.nn.silu(gate_pre) * up_pre)
        produced = low_back(low(jnp.dot(activated, down_weight, precision=highest)))
        return (running + column[:, None] * produced, None)
    routed, unused = lax.scan(jax.checkpoint(one_expert), jnp.zeros_like(middle), (expert_gate, expert_up, expert_down, route_weight.T))
    return middle + shared_branch + routed

def reference(tokens, cotangent, expert_ids, keep, gates, norm1_gain, norm2_gain, w_query, w_key, w_value, w_out, shared_gate, shared_up, shared_down, expert_gate, expert_up, expert_down):
    weights = tuple((item.astype(jnp.float32) for item in (norm1_gain, norm2_gain, w_query, w_key, w_value, w_out, shared_gate, shared_up, shared_down, expert_gate, expert_up, expert_down)))

    def per_sequence(totals, inputs):
        seq_tokens, seq_cot, seq_ids, seq_keep, seq_gates = inputs
        chosen = (seq_ids[:, :, None] == jnp.arange(EXPERTS, dtype=jnp.int32)[None, None, :]).astype(jnp.float32)
        route_weight = lax.optimization_barrier(jnp.sum(chosen * (seq_gates * seq_keep.astype(jnp.float32))[:, :, None], axis=1))

        def layer_of(*operands):
            return layer(*operands, route_weight)
        produced, pullback = jax.vjp(layer_of, seq_tokens.astype(jnp.float32), *weights)
        grads = pullback(seq_cot.astype(jnp.float32))
        updated = tuple((old + new for old, new in zip(totals, grads[1:])))
        return (updated, (produced.astype(jnp.bfloat16), grads[0]))
    initial = tuple((jnp.zeros_like(item) for item in weights))
    sums, (outputs, grad_input) = lax.scan(per_sequence, initial, (tokens, cotangent, expert_ids, keep, gates))
    return (outputs, grad_input, sums[0], sums[1], sums[2], sums[3], sums[4], sums[5], sums[6], sums[7], sums[8], sums[9], sums[10], sums[11])
```

```python
import math

import jax
import jax.numpy as jnp
from jax import lax
from jax.experimental import pallas as pl
from jax.experimental.pallas import tpu as pltpu
from jax.sharding import PartitionSpec as P

HEADS = 10
HEAD = 128
MAIN = 8
epsilon = 1e-06
negative = -1e30
bf16 = jnp.bfloat16
f32 = jnp.float32
VMEM_LIMIT = 64 * 1024 * 1024 - 128 * 1024


def dot(a, b):
    return jnp.dot(a, b, preferred_element_type=f32)


def dot_nt(a, b):
    return lax.dot_general(a, b, (((1,), (1,)), ((), ())), preferred_element_type=f32)


def dot_tn(a, b):
    return lax.dot_general(a, b, (((0,), (0,)), ((), ())), preferred_element_type=f32)


def tie(*values):
    return lax.optimization_barrier(values)


def after(value, *others):
    return lax.optimization_barrier((value, others))[0]


def cycle_of(size):
    if size == 16:
        return [0, 1, 2, 3, 7, 6, 5, 9, 10, 11, 15, 14, 13, 12, 8, 4]
    return list(range(0, size, 2)) + list(range(size - 1, 0, -2))


def spec(shape, index, single=False):
    if single:
        return pl.BlockSpec(shape, index, pipeline_mode=pl.Buffered(1))
    return pl.BlockSpec(shape, index)


class Ring:
    def __init__(self, size):
        self.size = size
        self.half = size // 2
        self.order = cycle_of(size)
        place = [0] * size
        for at, member in enumerate(self.order):
            place[member] = at
        self.forward = [(self.order[i], self.order[(i + 1) % size]) for i in range(size)]
        self.backward = [(self.order[i], self.order[(i - 1) % size]) for i in range(size)]
        self.place = jnp.array(place, jnp.int32)[lax.axis_index("ep")]

    def member(self, offset):
        return jnp.array(self.order, jnp.int32)[(self.place + offset) % self.size]

    def step(self, up, down, number):
        if number == self.half:
            cut = up.shape[0] // 2
            up, down = up[:cut], down[cut:]
        return lax.ppermute(up, "ep", self.forward), lax.ppermute(down, "ep", self.backward)

    def gather(self, own, visit):
        up, down, arrived, done = own, own, (own,), None
        for step in range(1, self.half + 1):
            if done is not None:
                up, down, done = lax.optimization_barrier((up, down, done))
            up, down = self.step(up, down, step)
            done = visit(step - 1, arrived)
            arrived = (up, down)
        visit(self.half, arrived)

    def scatter_step(self, parts, came, number):
        cut = parts[0].shape[0] // 2
        away = self.half - number + 1
        if number == 1:
            up, down = parts[away][:cut], parts[away][cut:]
        else:
            ahead, behind = parts[away], parts[-away]
            up, down = came
            if number == 2:
                up = jnp.concatenate([(ahead[:cut].astype(f32) + up.astype(f32)).astype(bf16), ahead[cut:]], axis=0)
                down = jnp.concatenate([behind[:cut], (behind[cut:].astype(f32) + down.astype(f32)).astype(bf16)], axis=0)
            else:
                up = (ahead.astype(f32) + up.astype(f32)).astype(bf16)
                down = (behind.astype(f32) + down.astype(f32)).astype(bf16)
        return lax.ppermute(up, "ep", self.forward), lax.ppermute(down, "ep", self.backward)

    def scatter_end(self, parts, came):
        return parts[0].astype(f32) + came[0].astype(f32) + came[1].astype(f32)


def qkv_kernel(base_ref, tok_ref, gain_ref, w_ref, cos_ref, sin_ref, *rest):
    hid_ref, qkv_ref = rest[-2:]
    x = tok_ref[...].astype(f32)
    inverse = lax.rsqrt(jnp.mean(x * x, axis=-1, keepdims=True) + epsilon)
    hidden = (x * inverse * gain_ref[...]).astype(bf16)
    hid_ref[...] = hidden
    out = dot(hidden, w_ref[...])
    cosine, sine = cos_ref[...], sin_ref[...]
    for slot in range(6):
        u = out[:, slot * HEAD : (slot + 1) * HEAD]
        if slot % 3 != 2:
            u = u * cosine + pltpu.roll(u, HEAD // 2, 1) * sine
        qkv_ref[:, slot * HEAD : (slot + 1) * HEAD] = u.astype(bf16)


def qkv_piece(base, piece, tile, gain, w_cat, cosine, sine, buffers):
    rows, width = piece.shape
    length = cosine.shape[0]
    cols = w_cat.shape[1]
    aliased = () if buffers is None else tuple(buffers)
    n_in = 6
    return pl.pallas_call(
        qkv_kernel,
        out_shape=(jax.ShapeDtypeStruct((length, width), bf16), jax.ShapeDtypeStruct((length, cols), bf16)),
        grid_spec=pltpu.PrefetchScalarGridSpec(
            num_scalar_prefetch=1,
            grid=(rows // tile,),
            in_specs=[
                pl.BlockSpec((tile, width), lambda i, b: (i, 0)),
                pl.BlockSpec((1, width), lambda i, b: (0, 0)),
                pl.BlockSpec((width, cols), lambda i, b: (0, 0)),
                pl.BlockSpec((tile, HEAD), lambda i, b: (b[0] + i, 0)),
                pl.BlockSpec((tile, HEAD), lambda i, b: (b[0] + i, 0)),
            ]
            + [pl.BlockSpec(memory_space=pl.ANY)] * len(aliased),
            out_specs=[
                pl.BlockSpec((tile, width), lambda i, b: (b[0] + i, 0)),
                pl.BlockSpec((tile, cols), lambda i, b: (b[0] + i, 0)),
            ],
        ),
        input_output_aliases={n_in + i: i for i in range(len(aliased))},
        compiler_params=pltpu.CompilerParams(vmem_limit_bytes=32 * 1024 * 1024),
        cost_estimate=pl.CostEstimate(
            flops=2 * rows * width * cols, bytes_accessed=4 * rows * width + 2 * (rows + width) * cols, transcendentals=0
        ),
        name="norm_project_rotate",
    )(base, piece, gain, w_cat, cosine, sine, *aliased)


def attention_forward(own, qkv, blocks, rows, main_rows, side_rows):
    scale = math.log2(math.e) / math.sqrt(HEAD)
    length = qkv.shape[0]
    tall = main_rows + side_rows

    def kernel(own_ref, qkv_ref, low_ref, att_ref, lse_ref):
        block = pl.program_id(0)

        def piece(col, offset, count):
            first = pl.multiple_of(block * rows + offset, 32)
            return qkv_ref[pl.ds(first, count), col : col + HEAD]

        offsets = (own_ref[0], own_ref[1])
        counts = (main_rows, side_rows)
        queries = [piece(3 * HEAD * i, offsets[i], counts[i]) for i in range(2)]

        def step(i, at, state, diagonal):
            best, total, acc = state
            first = pl.multiple_of(at * rows, rows)
            col = 3 * HEAD * i
            keys = qkv_ref[pl.ds(first, rows), col + HEAD : col + 2 * HEAD]
            values = qkv_ref[pl.ds(first, rows), col + 2 * HEAD : col + 3 * HEAD]
            scores = dot_nt(queries[i], keys) * scale
            if diagonal:
                q_at = lax.broadcasted_iota(jnp.int32, scores.shape, 0) + offsets[i]
                k_at = lax.broadcasted_iota(jnp.int32, scores.shape, 1)
                scores = jnp.where(q_at >= k_at, scores, negative)
            top = jnp.maximum(best, jnp.max(scores, axis=1, keepdims=True))
            weights = jnp.exp2(scores - top)
            factor = jnp.exp2(best - top)
            total = total * factor + jnp.sum(weights, axis=1, keepdims=True)
            acc = acc * factor + dot(weights.astype(bf16), values)
            return top, total, acc

        def both(at, states, diagonal=False):
            return tuple(step(i, at, states[i], diagonal) for i in range(2))

        start = tuple(
            (jnp.full((c, 1), negative, f32), jnp.zeros((c, 1), f32), jnp.zeros((c, HEAD), f32)) for c in counts
        )
        states = lax.fori_loop(0, block, both, start)
        states = both(block, states, True)
        at = 0
        for i in range(2):
            best, total, acc = states[i]
            attended = acc / total
            low_ref[0, at : at + counts[i]] = attended.astype(bf16)
            att_ref[0, at : at + counts[i]] = attended
            lse = jnp.broadcast_to(best + jnp.log2(total), (counts[i], HEAD))
            lse_ref[0, :, at : at + counts[i]] = jnp.transpose(lse)[0:8]
            at += counts[i]

    return pl.pallas_call(
        kernel,
        out_shape=(
            jax.ShapeDtypeStruct((blocks, tall, HEAD), bf16),
            jax.ShapeDtypeStruct((blocks, tall, HEAD), f32),
            jax.ShapeDtypeStruct((blocks, 8, tall), f32),
        ),
        grid_spec=pltpu.PrefetchScalarGridSpec(
            num_scalar_prefetch=1,
            grid=(blocks,),
            in_specs=[spec((length, qkv.shape[1]), lambda s, o: (0, 0), True)],
            out_specs=[
                pl.BlockSpec((1, tall, HEAD), lambda s, o: (s, 0, 0)),
                pl.BlockSpec((1, tall, HEAD), lambda s, o: (s, 0, 0)),
                pl.BlockSpec((1, 8, tall), lambda s, o: (s, 0, 0)),
            ],
        ),
        compiler_params=pltpu.CompilerParams(vmem_limit_bytes=48 * 1024 * 1024),
        cost_estimate=pl.CostEstimate(
            flops=4 * length * tall * blocks * HEAD // 2, bytes_accessed=16 * length * HEAD, transcendentals=length * tall * blocks // 2
        ),
        name="attention_forward",
    )(own, qkv)


def attention_backward(own, qkv, grads, attended, lse, cosine, sine, blocks, rows, count, slot, start):
    scale = 1.0 / math.sqrt(HEAD)
    scale_two = math.log2(math.e) * scale
    length = qkv.shape[0]
    tall = grads.shape[1]
    cols = 3 * HEAD
    here = slice(start, start + count)

    def kernel(own_ref, qkv_ref, grad_ref, att_ref, lse_ref, cos_ref, sin_ref, out_ref, key_sum, value_sum):
        block = pl.program_id(0)
        offset = own_ref[slot]

        @pl.when(block == 0)
        def _():
            key_sum[...] = jnp.zeros_like(key_sum)
            value_sum[...] = jnp.zeros_like(value_sum)
            if count < rows:
                out_ref[:, :HEAD] = jnp.zeros((length, HEAD), bf16)

        mine = pl.multiple_of(block * rows + offset, 32)
        queries = qkv_ref[pl.ds(mine, count), :HEAD]
        grad = grad_ref[0, here]
        lse_row = lse_ref[0, 0:1, here]
        product = grad.astype(f32) * att_ref[0, here]
        delta = jnp.sum(jnp.transpose(product), axis=0, keepdims=True)

        def step(at, dq, diagonal=False):
            first = pl.multiple_of(at * rows, rows)
            keys = qkv_ref[pl.ds(first, rows), HEAD : 2 * HEAD]
            values = qkv_ref[pl.ds(first, rows), 2 * HEAD :]
            scores = dot_nt(keys, queries) * scale_two
            if diagonal:
                k_at = lax.broadcasted_iota(jnp.int32, scores.shape, 0)
                q_at = lax.broadcasted_iota(jnp.int32, scores.shape, 1) + offset
                scores = jnp.where(q_at >= k_at, scores, negative)
            probs = jnp.exp2(scores - lse_row)
            grad_probs = dot_nt(values, grad)
            grad_scores = (probs * (grad_probs - delta)).astype(bf16)
            value_sum[pl.ds(first, rows)] += dot(probs.astype(bf16), grad)
            key_sum[pl.ds(first, rows)] += dot(grad_scores, queries)
            return dq + dot_tn(grad_scores, keys)

        dq = step(block, lax.fori_loop(0, block, step, jnp.zeros((count, HEAD), f32)), True)

        def turn_back(value, first, size):
            cosine_part = cos_ref[pl.ds(first, size)]
            sine_part = sin_ref[pl.ds(first, size)]
            value = value * scale
            return (value * cosine_part - pltpu.roll(value, HEAD // 2, 1) * sine_part).astype(bf16)

        out_ref[pl.ds(mine, count), :HEAD] = turn_back(dq, mine, count)

        @pl.when(block == blocks - 1)
        def _():
            def finish(at, carry):
                first = pl.multiple_of(at * rows, rows)
                out_ref[pl.ds(first, rows), HEAD : 2 * HEAD] = turn_back(key_sum[pl.ds(first, rows)], first, rows)
                out_ref[pl.ds(first, rows), 2 * HEAD :] = value_sum[pl.ds(first, rows)].astype(bf16)
                return carry

            lax.fori_loop(0, blocks, finish, 0)

    return pl.pallas_call(
        kernel,
        out_shape=jax.ShapeDtypeStruct((length, cols), bf16),
        grid_spec=pltpu.PrefetchScalarGridSpec(
            num_scalar_prefetch=1,
            grid=(blocks,),
            in_specs=[
                spec((length, cols), lambda s, o: (0, slot), True),
                pl.BlockSpec((1, tall, HEAD), lambda s, o: (s, 0, 0)),
                pl.BlockSpec((1, tall, HEAD), lambda s, o: (s, 0, 0)),
                pl.BlockSpec((1, 8, tall), lambda s, o: (s, 0, 0)),
                spec((length, HEAD), lambda s, o: (0, 0), True),
                spec((length, HEAD), lambda s, o: (0, 0), True),
            ],
            out_specs=spec((length, cols), lambda s, o: (0, 0), True),
            scratch_shapes=[pltpu.VMEM((length, HEAD), f32)] * 2,
        ),
        compiler_params=pltpu.CompilerParams(vmem_limit_bytes=40 * 1024 * 1024),
        cost_estimate=pl.CostEstimate(
            flops=10 * length * count * blocks * HEAD // 2, bytes_accessed=20 * length * HEAD, transcendentals=length * count * blocks // 2
        ),
        name="attention_backward",
    )(own, qkv, grads, attended, lse, cosine, sine)


def expert_call(sources, hidden, grads, rank_row, rank_col, route, w_gate, w_up, w_down, capacity, first, total, buffers):
    count = len(hidden)
    rows, width = hidden[0].shape
    local, _, inner = w_gate.shape
    aliased = () if buffers is None else tuple(buffers)
    widths = (width, width, inner, inner, inner)

    def kernel(sources_ref, *refs):
        h_refs, z_refs, row_refs, col_refs, gate_refs = (refs[i * count : (i + 1) * count] for i in range(5))
        wg_ref, wu_ref, wd_ref = refs[5 * count : 5 * count + 3]
        rest = refs[5 * count + 3 + len(aliased) :]
        outs_y, outs_x = rest[:count], rest[count : 2 * count]
        x_ref, dy_ref, a_ref, dg_ref, du_ref, keep_y, keep_x = rest[2 * count :]
        expert = pl.program_id(0)
        for p in range(count):
            slots = lax.broadcasted_iota(jnp.int32, (capacity, rows), 0).astype(f32)
            hit = slots == row_refs[p][0, expert]
            pick = jnp.where(hit, 1.0, 0.0).astype(bf16)
            gate = jnp.sum(jnp.where(hit, gate_refs[p][0, expert], 0.0), axis=1, keepdims=True)
            x = dot(pick, h_refs[p][...]).astype(bf16)
            dy = (dot(pick, z_refs[p][...]) * gate).astype(bf16)
            x_ref[0, p] = x
            dy_ref[0, p] = dy
            g = dot(x, wg_ref[0])
            u = dot(x, wu_ref[0])
            sigma = 1.0 / (1.0 + jnp.exp(-g))
            act = g * sigma
            a = (act * u).astype(bf16)
            a_ref[0, p] = a
            da = dot_nt(dy, wd_ref[0])
            du = (da * act).astype(bf16)
            dg = (da * u * sigma * (1.0 + g * (1.0 - sigma))).astype(bf16)
            du_ref[0, p] = du
            dg_ref[0, p] = dg
            y = dot(a, wd_ref[0]).astype(bf16)
            at = pl.multiple_of(expert * capacity, 16)
            keep_y[p, pl.ds(at, capacity)] = (y.astype(f32) * gate).astype(bf16)
            dx = dot_nt(dg, wg_ref[0]) + dot_nt(du, wu_ref[0])
            keep_x[p, pl.ds(at, capacity)] = dx.astype(bf16)

        @pl.when(expert == local - 1)
        def _():
            for p in range(count):
                slots = lax.broadcasted_iota(jnp.int32, (rows, capacity), 1).astype(f32)
                place = jnp.concatenate(
                    [jnp.where(slots == col_refs[p][0, e], 1.0, 0.0).astype(bf16) for e in range(local)], axis=1
                )
                outs_y[p][...] = dot(place, keep_y[p]).astype(bf16)
                outs_x[p][...] = dot(place, keep_x[p]).astype(bf16)

    piece = jax.ShapeDtypeStruct((rows, width), bf16)
    by_expert = lambda e, s: (e, 0, 0)
    slot = lambda e, s: (e, first // count, 0, 0)

    def of_source(shape):
        zeros = (0,) * (len(shape) - 1)
        return [pl.BlockSpec(shape, lambda e, s, p=p: (s[p],) + zeros, pipeline_mode=pl.Buffered(1)) for p in range(count)]

    return pl.pallas_call(
        kernel,
        out_shape=[piece] * (2 * count) + [jax.ShapeDtypeStruct((local, total, capacity, w), bf16) for w in widths],
        grid_spec=pltpu.PrefetchScalarGridSpec(
            num_scalar_prefetch=1,
            grid=(local,),
            in_specs=[spec((rows, width), lambda e, s: (0, 0), True)] * (2 * count)
            + of_source((1, local, 1, rows))
            + of_source((1, local, rows, 1))
            + of_source((1, local, 1, rows))
            + [
                pl.BlockSpec((1, width, inner), by_expert),
                pl.BlockSpec((1, width, inner), by_expert),
                pl.BlockSpec((1, inner, width), by_expert),
            ]
            + [pl.BlockSpec(memory_space=pl.ANY)] * len(aliased),
            out_specs=[spec((rows, width), lambda e, s: (0, 0), True)] * (2 * count)
            + [pl.BlockSpec((1, count, capacity, w), slot) for w in widths],
            scratch_shapes=[pltpu.VMEM((count, local * capacity, width), bf16)] * 2,
        ),
        input_output_aliases={1 + 5 * count + 3 + i: 2 * count + i for i in range(len(aliased))},
        compiler_params=pltpu.CompilerParams(vmem_limit_bytes=VMEM_LIMIT),
        cost_estimate=pl.CostEstimate(
            flops=count * 2 * local * capacity * width * (6 * inner + 4 * rows),
            bytes_accessed=2 * local * (3 * width * inner + count * capacity * (2 * width + 3 * inner)) + count * 8 * rows * width,
            transcendentals=count * local * capacity * inner,
        ),
        name="experts",
    )(
        sources,
        *hidden,
        *grads,
        *[rank_row] * count,
        *[rank_col] * count,
        *[route] * count,
        w_gate,
        w_up,
        w_down,
        *aliased,
    )


def swiglu_back(grad_act, gate_pre, up_pre):
    sigma = jax.nn.sigmoid(gate_pre)
    grad_up = (grad_act * gate_pre * sigma).astype(bf16)
    grad_gate = (grad_act * up_pre * sigma * (1.0 + gate_pre * (1.0 - sigma))).astype(bf16)
    return grad_gate, grad_up


def shards(
    tokens, cotangent, expert_ids, keep, gates, norm1_gain, norm2_gain, w_query, w_key, w_value, w_out,
    shared_gate, shared_up, shared_down, expert_gate, expert_up, expert_down,
):
    ep = lax.axis_size("ep")
    me = lax.axis_index("ep")
    ring = Ring(ep)
    half = ring.half
    token_rows = tokens[0]
    grad_low = cotangent[0]
    rows, width = token_rows.shape
    length = rows * ep
    local = expert_gate.shape[0]
    inner = expert_gate.shape[2]
    experts = local * ep
    shard = w_query.shape[0]
    copies = ep // MAIN
    sharers = MAIN // (HEADS - MAIN)
    main_rows = rows // copies
    side_rows = rows // (sharers * copies)
    tall = main_rows + side_rows
    capacity = min(rows, rows * 10 // experts)
    main_part = me % copies
    side_part = ((me // copies) % sharers) * copies + main_part
    own = jnp.stack([main_part * main_rows, side_part * side_rows]).astype(jnp.int32)

    gains = jnp.concatenate([norm1_gain[:, None], norm2_gain[:, None], jnp.zeros((shard, HEAD - 2), bf16)], axis=1)
    messages = []
    for member in range(ep):
        main_head = member // copies
        side_head = MAIN + main_head // sharers
        messages.append(
            jnp.concatenate(
                [
                    weight[:, head * HEAD : (head + 1) * HEAD]
                    for head in (main_head, side_head)
                    for weight in (w_query, w_key, w_value)
                ]
                + [gains],
                axis=1,
            )
        )
    head_rows = lax.all_to_all(jnp.stack(messages), "ep", 0, 0, tiled=True)

    chosen = expert_ids[0][:, :, None] == jnp.arange(experts, dtype=jnp.int32)[None, None, :]
    weight_here = gates[0] * keep[0].astype(f32)
    route = jnp.sum(jnp.where(chosen, weight_here[:, :, None], 0.0), axis=1)
    route = lax.all_to_all(route.T.reshape(ep, local, rows), "ep", 0, 0, tiled=True)
    used = route > 0.0
    before = (jnp.arange(rows)[:, None] < jnp.arange(rows)[None, :]).astype(bf16)
    rank = dot(used.astype(bf16).reshape(ep * local, rows), before).reshape(ep, local, rows)
    rank = jnp.where(used, rank, -1.0)

    freqs = jnp.exp(jnp.arange(HEAD // 2, dtype=f32) * (-2.0 * math.log(10000.0) / HEAD))
    turned = jnp.arange(length, dtype=jnp.int32).astype(f32)[:, None] * freqs[None, :]
    cosine, sine = jnp.cos(turned), jnp.sin(turned)
    cosine = jnp.concatenate([cosine, cosine], axis=1)
    sine = jnp.concatenate([-sine, sine], axis=1)

    tile = rows // 2
    arrivals, known = [], {}

    def project(steps):
        for step in steps:
            for i, part in enumerate(arrivals[step]):
                offset = 0 if step == 0 else (half if step == half else (-step, step)[i])
                base = 2 * ring.member(offset) + (i if step == half else 0)
                known["buffers"] = qkv_piece(
                    base.astype(jnp.int32).reshape(1), part, tile, known["gains"][0], known["w_cat"], cosine, sine,
                    known.get("buffers"),
                )

    up, down = token_rows, token_rows
    arrivals.append((token_rows,))
    for step in range(1, half + 1):
        up, down = ring.step(up, down, step)
        if step == 1:
            head_rows, up, down = tie(head_rows, up, down)
            head_weights = lax.all_gather(head_rows.reshape(ep * shard, 7 * HEAD), "dp", axis=0, tiled=True)
            gain_rows = head_weights[:, 6 * HEAD : 6 * HEAD + 2].astype(f32).T
            gain_one, gain_two = gain_rows[0:1], gain_rows[1:2]
            w_cat = head_weights[:, : 6 * HEAD]
            known["gains"], known["w_cat"] = (gain_one, gain_two), w_cat
        if step == 2:
            route, rank, up, down = tie(route, rank, up, down)
        if step == half - 1:
            project(range(half - 1))
            packed = jnp.concatenate([w_out, shared_gate, shared_up, shared_down.T], axis=1)
            up, down, packed, known["buffers"] = tie(up, down, packed, known["buffers"])
            packed = lax.all_gather(packed, "ep", axis=0, tiled=True)
        arrivals.append((up, down))
    project([half - 1, half])
    hidden_all, qkv = known["buffers"]

    grad_pieces = {0: (grad_low,)}
    grad_low, qkv = tie(grad_low, qkv)
    grad_pieces[1] = ring.step(grad_low, grad_low, 1)

    low, attended, lse = attention_forward(own, qkv, ep, rows, main_rows, side_rows)
    low, grad_pieces[1], packed = tie(low, grad_pieces[1], packed)
    full_out = lax.all_gather(packed[:, :width], "dp", axis=0, tiled=True)
    grad_pieces[2] = ring.step(*grad_pieces[1], 2)
    heads_in = lax.all_to_all(low, "ep", 0, 0, tiled=True)
    main_in = heads_in[:, :main_rows].reshape(MAIN, rows, HEAD)
    side_in = heads_in[:, main_rows:].reshape(HEADS - MAIN, rows, HEAD)
    attended_low = jnp.concatenate([main_in, side_in], axis=0).transpose(1, 0, 2).reshape(rows, width)

    residual = token_rows.astype(f32)
    middle = residual + dot(attended_low, full_out)
    inverse_two = lax.rsqrt(jnp.mean(middle * middle, axis=-1, keepdims=True) + epsilon)
    normed_two = middle * inverse_two
    hidden_two = (normed_two * gain_two).astype(bf16)

    hidden_two, grad_pieces[2], packed = tie(hidden_two, grad_pieces[2], packed)
    packed = lax.all_gather(packed[:, width:], "dp", axis=0, tiled=True)
    full_gate = packed[:, :inner]
    full_up = packed[:, inner : 2 * inner]
    full_down_t = packed[:, 2 * inner :]

    rank_row, rank_col, route_row = rank[:, :, None, :], rank[:, :, :, None], route[:, :, None, :]
    part_y, part_x, buffers = {}, {}, [None]

    def run_experts(step, arrived):
        grads = grad_pieces[step]
        if step == half:
            group, first = (half,), ep - 1
        elif step == 0:
            group, first = (0,), ep - 2
        else:
            group, first = (-step, step), 2 * (step - 1)
        outs = expert_call(
            jnp.stack([ring.member(offset) for offset in group]).astype(jnp.int32),
            arrived,
            grads,
            rank_row,
            rank_col,
            route_row,
            expert_gate,
            expert_up,
            expert_down,
            capacity,
            first,
            ep,
            buffers[0],
        )
        for i, offset in enumerate(group):
            part_y[offset] = outs[i]
            part_x[offset] = outs[len(group) + i]
        buffers[0] = outs[2 * len(group) :]
        return outs[len(group)]

    def run_shared(hidden, grads):
        gate_pre = dot(hidden, full_gate)
        up_pre = dot(hidden, full_up)
        act = (jax.nn.silu(gate_pre) * up_pre).astype(bf16)
        grad_gate_pre, grad_up_pre = swiglu_back(dot(grads, full_down_t), gate_pre, up_pre)
        back = dot_nt(grad_gate_pre, full_gate) + dot_nt(grad_up_pre, full_up)
        grads_in = dot_tn(hidden, jnp.concatenate([grad_gate_pre, grad_up_pre], axis=1)).astype(bf16)
        return dot_nt(act, full_down_t), back, grads_in, dot_tn(grads, act).astype(bf16)

    up, down, arrived = hidden_two, hidden_two, (hidden_two,)
    for step in range(1, half + 1):
        if step < half:
            up, down = ring.step(up, down, step)
            if step >= 4:
                grad_pieces[step] = ring.step(*grad_pieces[step - 1], step)
        else:
            up = lax.ppermute(up, "ep", ring.forward)
            grad_pieces[step] = (lax.ppermute(grad_pieces[step - 1][1], "ep", ring.backward),)
        done = run_experts(step - 1, arrived)
        up, down, done, grad_pieces[step] = tie(up, down, done, grad_pieces[step])
        if step == 2:
            hidden_two, grad_low, done = tie(hidden_two, grad_low, done)
            shared = run_shared(hidden_two, grad_low)
            arrived = (up, down)
            if half > 3:
                grad_pieces[3] = ring.step(*grad_pieces[2], 3)
                grad_pieces[3], done, shared, arrived = tie(grad_pieces[3], done, shared, arrived)
            else:
                done, shared, arrived = tie(done, shared, arrived)
            dense = [lax.psum_scatter(item, "dp", scatter_dimension=0, tiled=True) for item in shared[2:]]
        else:
            arrived = (up, down) if step < half else (up,)
        if step == half:
            done, dense = tie(done, dense)
        part_x[(0 if step == 1 else 1 - step)] = done
    run_experts(half, arrived)
    shared_branch, grad_shared = shared[:2]
    saved_x, saved_dy, saved_a, saved_dg, saved_du = [
        item.reshape(local, ep * capacity, item.shape[-1]) for item in buffers[0]
    ]

    def by_rows(left, right):
        return jnp.einsum("ecd,ecf->edf", left, right, preferred_element_type=f32).astype(bf16)

    came, expert_grads = None, []
    for step in range(1, half + 1):
        came = ring.scatter_step(part_x, came, step)
        if step <= 3:
            left, right = ((saved_x, saved_dg), (saved_x, saved_du), (saved_dy, saved_a))[step - 1]
            item = by_rows(left, right)
            came, item = tie(came, item)
            if step < 3:
                item = lax.psum_scatter(item, "dp", scatter_dimension=1, tiled=True)
            expert_grads.append(item)
    came, expert_grads[0] = tie(came, expert_grads[0])
    grad_routed = ring.scatter_end(part_x, came)
    grad_hidden_two = grad_shared + grad_routed
    grad_gain_two = jnp.sum(grad_hidden_two * normed_two, axis=0)
    scaled = grad_hidden_two * gain_two
    grad_out = grad_low.astype(f32)
    grad_middle = grad_out + inverse_two * (
        scaled - normed_two * jnp.mean(scaled * normed_two, axis=-1, keepdims=True)
    )
    grad_branch = grad_middle.astype(bf16)
    grad_attended = dot_nt(grad_branch, full_out).astype(bf16)

    by_head = grad_attended.reshape(rows, HEADS, HEAD).transpose(1, 0, 2)
    heads_out = jnp.concatenate(
        [by_head[:MAIN].reshape(ep, main_rows, HEAD), by_head[MAIN:].reshape(ep, side_rows, HEAD)], axis=1
    )
    part_y[half], grad_routed = tie(part_y[half], grad_routed)
    came_y = ring.scatter_step(part_y, None, 1)
    heads_out, attended_low, grad_branch, grad_gain_two, came_y = tie(
        heads_out, attended_low, grad_branch, grad_gain_two, came_y
    )
    came_y = ring.scatter_step(part_y, came_y, 2)
    head_grads = lax.all_to_all(heads_out, "ep", 0, 0, tiled=True)
    grad_full_out = dot_tn(attended_low, grad_branch).astype(bf16)

    gain_high = grad_gain_two.astype(bf16)
    gain_rest = (grad_gain_two - gain_high.astype(f32)).astype(bf16)
    gain_columns = dot_tn(jnp.stack([gain_high, gain_rest]), jnp.eye(2, HEAD, dtype=bf16))
    head_grads, came_y, grad_full_out, expert_grads[1] = tie(head_grads, came_y, grad_full_out, expert_grads[1])
    dense.append(lax.psum_scatter(grad_full_out, "dp", scatter_dimension=0, tiled=True))
    for step in range(3, half):
        came_y = ring.scatter_step(part_y, came_y, step)
    grad_side = attention_backward(
        own, qkv, head_grads, attended, lse, cosine, sine, ep, rows, side_rows, 1, main_rows
    )
    grad_side, came_y, qkv, dense = tie(grad_side, came_y, qkv, dense)
    dense = lax.psum_scatter(jnp.concatenate(dense, axis=1), "ep", scatter_dimension=0, tiled=True).astype(f32)
    came_y = ring.scatter_step(part_y, came_y, half)
    grad_main = attention_backward(
        own, qkv, head_grads, attended, lse, cosine, sine, ep, rows, main_rows, 0, 0
    )
    grad_main, came_y = tie(grad_main, came_y)

    part_h = {}
    for offset in range(-half + 1, half + 1):
        first = ring.member(offset) * rows
        part_h[offset] = (
            dot_nt(lax.dynamic_slice_in_dim(grad_main, first, rows, 0), w_cat[:, : 3 * HEAD])
            + dot_nt(lax.dynamic_slice_in_dim(grad_side, first, rows, 0), w_cat[:, 3 * HEAD :])
        ).astype(bf16)
    hidden_all, part_h[half] = tie(hidden_all, part_h[half])
    head_sums = jnp.concatenate([dot_tn(hidden_all, grad_main), dot_tn(hidden_all, grad_side), gain_columns], axis=1)
    head_sums = head_sums.astype(bf16)
    came = None
    for step in range(1, half + 1):
        came = ring.scatter_step(part_h, came, step)
        if step == 1:
            next_parts = [part_h[offset] for offset in (half - 1, 1 - half)]
            came, head_sums, next_parts = tie(came, head_sums, next_parts)
            part_h[half - 1], part_h[1 - half] = next_parts
            head_sums = lax.psum_scatter(head_sums, "dp", scatter_dimension=0, tiled=True)
        if step == 2:
            came, part_h = tie(came, part_h)
        if step == 3:
            came, head_sums, dense, last = tie(came, head_sums, dense, expert_grads[2])
            head_sums = lax.all_to_all(head_sums.reshape(ep, shard, 7 * HEAD), "ep", 0, 0, tiled=True)
            expert_grads[2] = lax.psum_scatter(last, "dp", scatter_dimension=1, tiled=True)
    head_sums = head_sums.astype(f32)
    grad_hidden_one = ring.scatter_end(part_h, came)
    output = (middle + shared_branch + ring.scatter_end(part_y, came_y)).astype(bf16)
    main_sums = head_sums[:, :, : 3 * HEAD].reshape(MAIN, copies, shard, 3, HEAD).sum(1)
    gain_sums = head_sums[:, :, 6 * HEAD] + head_sums[:, :, 6 * HEAD + 1]
    side_sums = head_sums[:, :, 3 * HEAD : 6 * HEAD].reshape(HEADS - MAIN, sharers * copies, shard, 3, HEAD).sum(1)
    head_sums = jnp.concatenate([main_sums, side_sums], axis=0)
    projections = [head_sums[:, :, i].transpose(1, 0, 2).reshape(shard, width) for i in range(3)]
    grad_gain_one = sum(
        jnp.sum(w.astype(f32) * g, axis=1) for w, g in zip((w_query, w_key, w_value), projections)
    ) / norm1_gain.astype(f32)

    inverse_one = lax.rsqrt(jnp.mean(residual * residual, axis=-1, keepdims=True) + epsilon)
    normed_one = residual * inverse_one
    scaled = grad_hidden_one * gain_one
    grad_input = grad_middle + inverse_one * (
        scaled - normed_one * jnp.mean(scaled * normed_one, axis=-1, keepdims=True)
    )
    return (
        output[None],
        grad_input[None],
        grad_gain_one,
        gain_sums.sum(0),
        projections[0],
        projections[1],
        projections[2],
        dense[:, 3 * inner : 3 * inner + width],
        dense[:, :inner],
        dense[:, inner : 2 * inner],
        dense[:, 2 * inner : 3 * inner].T,
        expert_grads[0].astype(f32),
        expert_grads[1].astype(f32),
        expert_grads[2].astype(f32).transpose(0, 2, 1),
    )


def solution(mesh):
    by_token = P("dp", "ep", None)
    by_row = P(("dp", "ep"), None)
    in_specs = (
        (by_token,) * 5
        + (P(("dp", "ep")),) * 2
        + (by_row,) * 6
        + (P(None, ("dp", "ep")),)
        + (P("ep", None, None),) * 3
    )
    out_specs = (
        (by_token,) * 2
        + (P(("dp", "ep")),) * 2
        + (by_row,) * 6
        + (P(None, ("dp", "ep")), P("ep", "dp", None), P("ep", "dp", None), P("ep", None, "dp"))
    )
    return jax.shard_map(shards, mesh=mesh, in_specs=in_specs, out_specs=out_specs, check_vma=False)
```

```python
import math

import jax
import jax.numpy as jnp
from jax import lax
from jax.experimental import pallas as pl
from jax.experimental.pallas import tpu as pltpu
from jax.sharding import PartitionSpec as P

HEADS = 10
HEAD = 128
MAIN = 8
epsilon = 1e-06
negative = -1e30
bf16 = jnp.bfloat16
f32 = jnp.float32
VMEM_LIMIT = 64 * 1024 * 1024 - 128 * 1024


def dot(a, b):
    return jnp.dot(a, b, preferred_element_type=f32)


def dot_nt(a, b):
    return lax.dot_general(a, b, (((1,), (1,)), ((), ())), preferred_element_type=f32)


def dot_tn(a, b):
    return lax.dot_general(a, b, (((0,), (0,)), ((), ())), preferred_element_type=f32)


def tie(*values):
    return lax.optimization_barrier(values)


def after(value, *others):
    return lax.optimization_barrier((value, others))[0]


def cycle_of(size):
    if size == 16:
        return [0, 1, 2, 3, 7, 6, 5, 9, 10, 11, 15, 14, 13, 12, 8, 4]
    return list(range(0, size, 2)) + list(range(size - 1, 0, -2))


def spec(shape, index, single=False):
    if single:
        return pl.BlockSpec(shape, index, pipeline_mode=pl.Buffered(1))
    return pl.BlockSpec(shape, index)


class Ring:
    def __init__(self, size):
        self.size = size
        self.half = size // 2
        self.order = cycle_of(size)
        place = [0] * size
        for at, member in enumerate(self.order):
            place[member] = at
        self.forward = [(self.order[i], self.order[(i + 1) % size]) for i in range(size)]
        self.backward = [(self.order[i], self.order[(i - 1) % size]) for i in range(size)]
        table = [[self.order[(place[me] + offset) % size] for offset in range(size)] for me in range(size)]
        self.members = lax.dynamic_index_in_dim(jnp.array(table, jnp.int32), lax.axis_index("ep"), 0, keepdims=False)

    def member(self, offset):
        return self.members[offset % self.size]

    def step(self, up, down, number):
        if number == self.half:
            cut = up.shape[0] // 2
            up, down = up[:cut], down[cut:]
        return lax.ppermute(up, "ep", self.forward), lax.ppermute(down, "ep", self.backward)

    def gather(self, own, visit):
        up, down, arrived, done = own, own, (own,), None
        for step in range(1, self.half + 1):
            if done is not None:
                up, down, done = lax.optimization_barrier((up, down, done))
            up, down = self.step(up, down, step)
            done = visit(step - 1, arrived)
            arrived = (up, down)
        visit(self.half, arrived)

    def scatter_step(self, parts, came, number):
        cut = parts[0].shape[0] // 2
        away = self.half - number + 1
        if number == 1:
            up, down = parts[away][:cut], parts[away][cut:]
        else:
            ahead, behind = parts[away], parts[-away]
            up, down = came
            if number == 2:
                up = jnp.concatenate([(ahead[:cut].astype(f32) + up.astype(f32)).astype(bf16), ahead[cut:]], axis=0)
                down = jnp.concatenate([behind[:cut], (behind[cut:].astype(f32) + down.astype(f32)).astype(bf16)], axis=0)
            else:
                up = (ahead.astype(f32) + up.astype(f32)).astype(bf16)
                down = (behind.astype(f32) + down.astype(f32)).astype(bf16)
        return lax.ppermute(up, "ep", self.forward), lax.ppermute(down, "ep", self.backward)

    def scatter_end(self, parts, came):
        return parts[0].astype(f32) + came[0].astype(f32) + came[1].astype(f32)


def qkv_kernel(members_ref, tok_ref, gain_ref, w_ref, cos_ref, sin_ref, *rest):
    hid_ref, qkv_ref = rest[-2:]
    x = tok_ref[...].astype(f32)
    inverse = lax.rsqrt(jnp.mean(x * x, axis=-1, keepdims=True) + epsilon)
    hidden = (x * inverse * gain_ref[...]).astype(bf16)
    hid_ref[...] = hidden
    out = dot(hidden, w_ref[...])
    cosine, sine = cos_ref[...], sin_ref[...]
    for slot in range(6):
        u = out[:, slot * HEAD : (slot + 1) * HEAD]
        if slot % 3 != 2:
            u = u * cosine + pltpu.roll(u, HEAD // 2, 1) * sine
        qkv_ref[:, slot * HEAD : (slot + 1) * HEAD] = u.astype(bf16)


def qkv_piece(members, offset, shift, piece, tile, gain, w_cat, cosine, sine, buffers):
    rows, width = piece.shape
    length = cosine.shape[0]
    cols = w_cat.shape[1]
    aliased = () if buffers is None else tuple(buffers)
    n_in = 6
    at = lambda i, m: (2 * m[offset] + shift + i, 0)
    return pl.pallas_call(
        qkv_kernel,
        out_shape=(jax.ShapeDtypeStruct((length, width), bf16), jax.ShapeDtypeStruct((length, cols), bf16)),
        grid_spec=pltpu.PrefetchScalarGridSpec(
            num_scalar_prefetch=1,
            grid=(rows // tile,),
            in_specs=[
                pl.BlockSpec((tile, width), lambda i, b: (i, 0)),
                pl.BlockSpec((1, width), lambda i, b: (0, 0)),
                pl.BlockSpec((width, cols), lambda i, b: (0, 0)),
                pl.BlockSpec((tile, HEAD), at),
                pl.BlockSpec((tile, HEAD), at),
            ]
            + [pl.BlockSpec(memory_space=pl.ANY)] * len(aliased),
            out_specs=[
                pl.BlockSpec((tile, width), at),
                pl.BlockSpec((tile, cols), at),
            ],
        ),
        input_output_aliases={n_in + i: i for i in range(len(aliased))},
        compiler_params=pltpu.CompilerParams(vmem_limit_bytes=32 * 1024 * 1024),
        cost_estimate=pl.CostEstimate(
            flops=2 * rows * width * cols, bytes_accessed=4 * rows * width + 2 * (rows + width) * cols, transcendentals=0
        ),
        name="norm_project_rotate",
    )(members, piece, gain, w_cat, cosine, sine, *aliased)


def attention_forward(own, qkv, blocks, rows, main_rows, side_rows):
    scale = math.log2(math.e) / math.sqrt(HEAD)
    length = qkv.shape[0]
    tall = main_rows + side_rows

    def kernel(own_ref, qkv_ref, low_ref, att_ref, lse_ref):
        block = pl.program_id(0)

        def piece(col, offset, count):
            first = pl.multiple_of(block * rows + offset, 32)
            return qkv_ref[pl.ds(first, count), col : col + HEAD]

        offsets = (own_ref[0], own_ref[1])
        counts = (main_rows, side_rows)
        queries = [piece(3 * HEAD * i, offsets[i], counts[i]) for i in range(2)]

        def step(i, at, state, diagonal):
            best, total, acc = state
            first = pl.multiple_of(at * rows, rows)
            col = 3 * HEAD * i
            keys = qkv_ref[pl.ds(first, rows), col + HEAD : col + 2 * HEAD]
            values = qkv_ref[pl.ds(first, rows), col + 2 * HEAD : col + 3 * HEAD]
            scores = dot_nt(queries[i], keys) * scale
            if diagonal:
                q_at = lax.broadcasted_iota(jnp.int32, scores.shape, 0) + offsets[i]
                k_at = lax.broadcasted_iota(jnp.int32, scores.shape, 1)
                scores = jnp.where(q_at >= k_at, scores, negative)
            top = jnp.maximum(best, jnp.max(scores, axis=1, keepdims=True))
            weights = jnp.exp2(scores - top)
            factor = jnp.exp2(best - top)
            total = total * factor + jnp.sum(weights, axis=1, keepdims=True)
            acc = acc * factor + dot(weights.astype(bf16), values)
            return top, total, acc

        def both(at, states, diagonal=False):
            return tuple(step(i, at, states[i], diagonal) for i in range(2))

        start = tuple(
            (jnp.full((c, 1), negative, f32), jnp.zeros((c, 1), f32), jnp.zeros((c, HEAD), f32)) for c in counts
        )
        states = lax.fori_loop(0, block, both, start)
        states = both(block, states, True)
        at = 0
        for i in range(2):
            best, total, acc = states[i]
            attended = acc / total
            low_ref[0, at : at + counts[i]] = attended.astype(bf16)
            att_ref[0, at : at + counts[i]] = attended
            lse = jnp.broadcast_to(best + jnp.log2(total), (counts[i], HEAD))
            lse_ref[0, :, at : at + counts[i]] = jnp.transpose(lse)[0:8]
            at += counts[i]

    return pl.pallas_call(
        kernel,
        out_shape=(
            jax.ShapeDtypeStruct((blocks, tall, HEAD), bf16),
            jax.ShapeDtypeStruct((blocks, tall, HEAD), f32),
            jax.ShapeDtypeStruct((blocks, 8, tall), f32),
        ),
        grid_spec=pltpu.PrefetchScalarGridSpec(
            num_scalar_prefetch=1,
            grid=(blocks,),
            in_specs=[spec((length, qkv.shape[1]), lambda s, o: (0, 0), True)],
            out_specs=[
                pl.BlockSpec((1, tall, HEAD), lambda s, o: (s, 0, 0)),
                pl.BlockSpec((1, tall, HEAD), lambda s, o: (s, 0, 0)),
                pl.BlockSpec((1, 8, tall), lambda s, o: (s, 0, 0)),
            ],
        ),
        compiler_params=pltpu.CompilerParams(vmem_limit_bytes=48 * 1024 * 1024),
        cost_estimate=pl.CostEstimate(
            flops=4 * length * tall * blocks * HEAD // 2, bytes_accessed=16 * length * HEAD, transcendentals=length * tall * blocks // 2
        ),
        name="attention_forward",
    )(own, qkv)


def attention_backward(own, qkv, grads, attended, lse, cosine, sine, blocks, rows, count, slot, start):
    scale = 1.0 / math.sqrt(HEAD)
    scale_two = math.log2(math.e) * scale
    length = qkv.shape[0]
    tall = grads.shape[1]
    cols = 3 * HEAD
    here = slice(start, start + count)

    def kernel(own_ref, qkv_ref, grad_ref, att_ref, lse_ref, cos_ref, sin_ref, out_ref, key_sum, value_sum):
        block = pl.program_id(0)
        offset = own_ref[slot]

        @pl.when(block == 0)
        def _():
            key_sum[...] = jnp.zeros_like(key_sum)
            value_sum[...] = jnp.zeros_like(value_sum)
            if count < rows:
                out_ref[:, :HEAD] = jnp.zeros((length, HEAD), bf16)

        mine = pl.multiple_of(block * rows + offset, 32)
        queries = qkv_ref[pl.ds(mine, count), :HEAD]
        grad = grad_ref[0, here]
        lse_row = lse_ref[0, 0:1, here]
        product = grad.astype(f32) * att_ref[0, here]
        delta = jnp.sum(jnp.transpose(product), axis=0, keepdims=True)

        def step(at, dq, diagonal=False):
            first = pl.multiple_of(at * rows, rows)
            keys = qkv_ref[pl.ds(first, rows), HEAD : 2 * HEAD]
            values = qkv_ref[pl.ds(first, rows), 2 * HEAD :]
            scores = dot_nt(keys, queries) * scale_two
            if diagonal:
                k_at = lax.broadcasted_iota(jnp.int32, scores.shape, 0)
                q_at = lax.broadcasted_iota(jnp.int32, scores.shape, 1) + offset
                scores = jnp.where(q_at >= k_at, scores, negative)
            probs = jnp.exp2(scores - lse_row)
            grad_probs = dot_nt(values, grad)
            grad_scores = (probs * (grad_probs - delta)).astype(bf16)
            value_sum[pl.ds(first, rows)] += dot(probs.astype(bf16), grad)
            key_sum[pl.ds(first, rows)] += dot(grad_scores, queries)
            return dq + dot_tn(grad_scores, keys)

        dq = step(block, lax.fori_loop(0, block, step, jnp.zeros((count, HEAD), f32)), True)

        def turn_back(value, first, size):
            cosine_part = cos_ref[pl.ds(first, size)]
            sine_part = sin_ref[pl.ds(first, size)]
            value = value * scale
            return (value * cosine_part - pltpu.roll(value, HEAD // 2, 1) * sine_part).astype(bf16)

        out_ref[pl.ds(mine, count), :HEAD] = turn_back(dq, mine, count)

        @pl.when(block == blocks - 1)
        def _():
            def finish(at, carry):
                first = pl.multiple_of(at * rows, rows)
                out_ref[pl.ds(first, rows), HEAD : 2 * HEAD] = turn_back(key_sum[pl.ds(first, rows)], first, rows)
                out_ref[pl.ds(first, rows), 2 * HEAD :] = value_sum[pl.ds(first, rows)].astype(bf16)
                return carry

            lax.fori_loop(0, blocks, finish, 0)

    return pl.pallas_call(
        kernel,
        out_shape=jax.ShapeDtypeStruct((length, cols), bf16),
        grid_spec=pltpu.PrefetchScalarGridSpec(
            num_scalar_prefetch=1,
            grid=(blocks,),
            in_specs=[
                spec((length, cols), lambda s, o: (0, slot), True),
                pl.BlockSpec((1, tall, HEAD), lambda s, o: (s, 0, 0)),
                pl.BlockSpec((1, tall, HEAD), lambda s, o: (s, 0, 0)),
                pl.BlockSpec((1, 8, tall), lambda s, o: (s, 0, 0)),
                spec((length, HEAD), lambda s, o: (0, 0), True),
                spec((length, HEAD), lambda s, o: (0, 0), True),
            ],
            out_specs=spec((length, cols), lambda s, o: (0, 0), True),
            scratch_shapes=[pltpu.VMEM((length, HEAD), f32)] * 2,
        ),
        compiler_params=pltpu.CompilerParams(vmem_limit_bytes=40 * 1024 * 1024),
        cost_estimate=pl.CostEstimate(
            flops=10 * length * count * blocks * HEAD // 2, bytes_accessed=20 * length * HEAD, transcendentals=length * count * blocks // 2
        ),
        name="attention_backward",
    )(own, qkv, grads, attended, lse, cosine, sine)


def expert_call(members, offsets, hidden, grads, rank_row, rank_col, route, w_gate, w_up, w_down, capacity, first, total, buffers):
    count = len(hidden)
    rows, width = hidden[0].shape
    local, _, inner = w_gate.shape
    aliased = () if buffers is None else tuple(buffers)
    widths = (width, width, inner, inner, inner)

    def kernel(members_ref, *refs):
        h_refs, z_refs, row_refs, col_refs, gate_refs = (refs[i * count : (i + 1) * count] for i in range(5))
        wg_ref, wu_ref, wd_ref = refs[5 * count : 5 * count + 3]
        rest = refs[5 * count + 3 + len(aliased) :]
        outs_y, outs_x = rest[:count], rest[count : 2 * count]
        x_ref, dy_ref, a_ref, dg_ref, du_ref, keep_y, keep_x = rest[2 * count :]
        expert = pl.program_id(0)
        for p in range(count):
            slots = lax.broadcasted_iota(jnp.int32, (capacity, rows), 0).astype(f32)
            hit = slots == row_refs[p][0, expert]
            pick = jnp.where(hit, 1.0, 0.0).astype(bf16)
            gate = jnp.sum(jnp.where(hit, gate_refs[p][0, expert], 0.0), axis=1, keepdims=True)
            x = dot(pick, h_refs[p][...]).astype(bf16)
            dy = (dot(pick, z_refs[p][...]) * gate).astype(bf16)
            x_ref[0, p] = x
            dy_ref[0, p] = dy
            g = dot(x, wg_ref[0])
            u = dot(x, wu_ref[0])
            sigma = 1.0 / (1.0 + jnp.exp(-g))
            act = g * sigma
            a = (act * u).astype(bf16)
            a_ref[0, p] = a
            da = dot_nt(dy, wd_ref[0])
            du = (da * act).astype(bf16)
            dg = (da * u * sigma * (1.0 + g * (1.0 - sigma))).astype(bf16)
            du_ref[0, p] = du
            dg_ref[0, p] = dg
            y = dot(a, wd_ref[0]).astype(bf16)
            at = pl.multiple_of(expert * capacity, 16)
            keep_y[p, pl.ds(at, capacity)] = (y.astype(f32) * gate).astype(bf16)
            dx = dot_nt(dg, wg_ref[0]) + dot_nt(du, wu_ref[0])
            keep_x[p, pl.ds(at, capacity)] = dx.astype(bf16)

        @pl.when(expert == local - 1)
        def _():
            for p in range(count):
                slots = lax.broadcasted_iota(jnp.int32, (rows, capacity), 1).astype(f32)
                place = jnp.concatenate(
                    [jnp.where(slots == col_refs[p][0, e], 1.0, 0.0).astype(bf16) for e in range(local)], axis=1
                )
                outs_y[p][...] = dot(place, keep_y[p]).astype(bf16)
                outs_x[p][...] = dot(place, keep_x[p]).astype(bf16)

    piece = jax.ShapeDtypeStruct((rows, width), bf16)
    by_expert = lambda e, s: (e, 0, 0)
    slot = lambda e, s: (e, first // count, 0, 0)

    def of_source(shape):
        zeros = (0,) * (len(shape) - 1)
        return [pl.BlockSpec(shape, lambda e, s, p=p: (s[offsets[p]],) + zeros, pipeline_mode=pl.Buffered(1)) for p in range(count)]

    return pl.pallas_call(
        kernel,
        out_shape=[piece] * (2 * count) + [jax.ShapeDtypeStruct((local, total, capacity, w), bf16) for w in widths],
        grid_spec=pltpu.PrefetchScalarGridSpec(
            num_scalar_prefetch=1,
            grid=(local,),
            in_specs=[spec((rows, width), lambda e, s: (0, 0), True)] * (2 * count)
            + of_source((1, local, 1, rows))
            + of_source((1, local, rows, 1))
            + of_source((1, local, 1, rows))
            + [
                pl.BlockSpec((1, width, inner), by_expert),
                pl.BlockSpec((1, width, inner), by_expert),
                pl.BlockSpec((1, inner, width), by_expert),
            ]
            + [pl.BlockSpec(memory_space=pl.ANY)] * len(aliased),
            out_specs=[spec((rows, width), lambda e, s: (0, 0), True)] * (2 * count)
            + [pl.BlockSpec((1, count, capacity, w), slot) for w in widths],
            scratch_shapes=[pltpu.VMEM((count, local * capacity, width), bf16)] * 2,
        ),
        input_output_aliases={1 + 5 * count + 3 + i: 2 * count + i for i in range(len(aliased))},
        compiler_params=pltpu.CompilerParams(vmem_limit_bytes=VMEM_LIMIT),
        cost_estimate=pl.CostEstimate(
            flops=count * 2 * local * capacity * width * (6 * inner + 4 * rows),
            bytes_accessed=2 * local * (3 * width * inner + count * capacity * (2 * width + 3 * inner)) + count * 8 * rows * width,
            transcendentals=count * local * capacity * inner,
        ),
        name="experts",
    )(
        members,
        *hidden,
        *grads,
        *[rank_row] * count,
        *[rank_col] * count,
        *[route] * count,
        w_gate,
        w_up,
        w_down,
        *aliased,
    )


def swiglu_back(grad_act, gate_pre, up_pre):
    sigma = jax.nn.sigmoid(gate_pre)
    grad_up = (grad_act * gate_pre * sigma).astype(bf16)
    grad_gate = (grad_act * up_pre * sigma * (1.0 + gate_pre * (1.0 - sigma))).astype(bf16)
    return grad_gate, grad_up


def shards(
    tokens, cotangent, expert_ids, keep, gates, norm1_gain, norm2_gain, w_query, w_key, w_value, w_out,
    shared_gate, shared_up, shared_down, expert_gate, expert_up, expert_down,
):
    ep = lax.axis_size("ep")
    me = lax.axis_index("ep")
    ring = Ring(ep)
    half = ring.half
    token_rows = tokens[0]
    grad_low = cotangent[0]
    rows, width = token_rows.shape
    length = rows * ep
    local = expert_gate.shape[0]
    inner = expert_gate.shape[2]
    experts = local * ep
    shard = w_query.shape[0]
    copies = ep // MAIN
    sharers = MAIN // (HEADS - MAIN)
    main_rows = rows // copies
    side_rows = rows // (sharers * copies)
    tall = main_rows + side_rows
    capacity = min(rows, rows * 10 // experts)
    main_part = me % copies
    side_part = ((me // copies) % sharers) * copies + main_part
    own = jnp.stack([main_part * main_rows, side_part * side_rows]).astype(jnp.int32)

    gains = jnp.concatenate([norm1_gain[:, None], norm2_gain[:, None], jnp.zeros((shard, HEAD - 2), bf16)], axis=1)
    messages = []
    for member in range(ep):
        main_head = member // copies
        side_head = MAIN + main_head // sharers
        messages.append(
            jnp.concatenate(
                [
                    weight[:, head * HEAD : (head + 1) * HEAD]
                    for head in (main_head, side_head)
                    for weight in (w_query, w_key, w_value)
                ]
                + [gains],
                axis=1,
            )
        )
    head_rows = lax.all_to_all(jnp.stack(messages), "ep", 0, 0, tiled=True)

    chosen = expert_ids[0][:, :, None] == jnp.arange(experts, dtype=jnp.int32)[None, None, :]
    weight_here = gates[0] * keep[0].astype(f32)
    route = jnp.sum(jnp.where(chosen, weight_here[:, :, None], 0.0), axis=1)
    route = lax.all_to_all(route.T.reshape(ep, local, rows), "ep", 0, 0, tiled=True)
    used = route > 0.0
    before = (jnp.arange(rows)[:, None] < jnp.arange(rows)[None, :]).astype(bf16)
    rank = dot(used.astype(bf16).reshape(ep * local, rows), before).reshape(ep, local, rows)
    rank = jnp.where(used, rank, -1.0)

    freqs = jnp.exp(jnp.arange(HEAD // 2, dtype=f32) * (-2.0 * math.log(10000.0) / HEAD))
    turned = jnp.arange(length, dtype=jnp.int32).astype(f32)[:, None] * freqs[None, :]
    cosine, sine = jnp.cos(turned), jnp.sin(turned)
    cosine = jnp.concatenate([cosine, cosine], axis=1)
    sine = jnp.concatenate([-sine, sine], axis=1)

    tile = rows // 2
    arrivals, known = [], {}

    def project(steps):
        for step in steps:
            for i, part in enumerate(arrivals[step]):
                offset = 0 if step == 0 else (half if step == half else (-step, step)[i])
                known["buffers"] = qkv_piece(
                    ring.members, offset % ep, i if step == half else 0, part, tile, known["gains"][0], known["w_cat"],
                    cosine, sine, known.get("buffers"),
                )

    up, down = token_rows, token_rows
    arrivals.append((token_rows,))
    for step in range(1, half + 1):
        up, down = ring.step(up, down, step)
        if step == 1:
            head_rows, up, down = tie(head_rows, up, down)
            head_weights = lax.all_gather(head_rows.reshape(ep * shard, 7 * HEAD), "dp", axis=0, tiled=True)
            gain_rows = head_weights[:, 6 * HEAD : 6 * HEAD + 2].astype(f32).T
            gain_one, gain_two = gain_rows[0:1], gain_rows[1:2]
            w_cat = head_weights[:, : 6 * HEAD]
            known["gains"], known["w_cat"] = (gain_one, gain_two), w_cat
        if step == 2:
            route, rank, up, down = tie(route, rank, up, down)
        if step == half - 1:
            project(range(half - 1))
            packed = jnp.concatenate([w_out, shared_gate, shared_up, shared_down.T], axis=1)
            up, down, packed, known["buffers"] = tie(up, down, packed, known["buffers"])
            packed = lax.all_gather(packed, "ep", axis=0, tiled=True)
        arrivals.append((up, down))
    project([half - 1, half])
    hidden_all, qkv = known["buffers"]

    grad_pieces = {0: (grad_low,)}
    grad_low, qkv = tie(grad_low, qkv)
    grad_pieces[1] = ring.step(grad_low, grad_low, 1)

    low, attended, lse = attention_forward(own, qkv, ep, rows, main_rows, side_rows)
    low, grad_pieces[1], packed = tie(low, grad_pieces[1], packed)
    full_out = lax.all_gather(packed[:, :width], "dp", axis=0, tiled=True)
    grad_pieces[2] = ring.step(*grad_pieces[1], 2)
    heads_in = lax.all_to_all(low, "ep", 0, 0, tiled=True)
    rank_row, rank_col, route_row = rank[:, :, None, :], rank[:, :, :, None], route[:, :, None, :]
    heads_in, rank_col = tie(heads_in, rank_col)
    main_in = heads_in[:, :main_rows].reshape(MAIN, rows, HEAD)
    side_in = heads_in[:, main_rows:].reshape(HEADS - MAIN, rows, HEAD)
    attended_low = jnp.concatenate([main_in, side_in], axis=0).transpose(1, 0, 2).reshape(rows, width)

    residual = token_rows.astype(f32)
    middle = residual + dot(attended_low, full_out)
    inverse_two = lax.rsqrt(jnp.mean(middle * middle, axis=-1, keepdims=True) + epsilon)
    normed_two = middle * inverse_two
    hidden_two = (normed_two * gain_two).astype(bf16)

    hidden_two, grad_pieces[2], packed = tie(hidden_two, grad_pieces[2], packed)
    packed = lax.all_gather(packed[:, width:], "dp", axis=0, tiled=True)
    full_gate = packed[:, :inner]
    full_up = packed[:, inner : 2 * inner]
    full_down_t = packed[:, 2 * inner :]

    part_y, part_x, buffers = {}, {}, [None]

    def run_experts(step, arrived):
        grads = grad_pieces[step]
        if step == half:
            group, first = (half,), ep - 1
        elif step == 0:
            group, first = (0,), ep - 2
        else:
            group, first = (-step, step), 2 * (step - 1)
        outs = expert_call(
            ring.members,
            [offset % ep for offset in group],
            arrived,
            grads,
            rank_row,
            rank_col,
            route_row,
            expert_gate,
            expert_up,
            expert_down,
            capacity,
            first,
            ep,
            buffers[0],
        )
        for i, offset in enumerate(group):
            part_y[offset] = outs[i]
            part_x[offset] = outs[len(group) + i]
        buffers[0] = outs[2 * len(group) :]
        return outs[len(group)]

    def run_shared(hidden, grads):
        gate_pre = dot(hidden, full_gate)
        up_pre = dot(hidden, full_up)
        act = (jax.nn.silu(gate_pre) * up_pre).astype(bf16)
        grad_gate_pre, grad_up_pre = swiglu_back(dot(grads, full_down_t), gate_pre, up_pre)
        back = dot_nt(grad_gate_pre, full_gate) + dot_nt(grad_up_pre, full_up)
        grads_in = dot_tn(hidden, jnp.concatenate([grad_gate_pre, grad_up_pre], axis=1)).astype(bf16)
        return dot_nt(act, full_down_t), back, grads_in, dot_tn(grads, act).astype(bf16)

    up, down, arrived = hidden_two, hidden_two, (hidden_two,)
    for step in range(1, half + 1):
        if step < half:
            up, down = ring.step(up, down, step)
            if step >= 4:
                grad_pieces[step] = ring.step(*grad_pieces[step - 1], step)
        else:
            up = lax.ppermute(up, "ep", ring.forward)
            grad_pieces[step] = (lax.ppermute(grad_pieces[step - 1][1], "ep", ring.backward),)
        done = run_experts(step - 1, arrived)
        up, down, done, grad_pieces[step] = tie(up, down, done, grad_pieces[step])
        if step == 2:
            hidden_two, grad_low, done = tie(hidden_two, grad_low, done)
            shared = run_shared(hidden_two, grad_low)
            arrived = (up, down)
            if half > 3:
                grad_pieces[3] = ring.step(*grad_pieces[2], 3)
                grad_pieces[3], done, shared, arrived = tie(grad_pieces[3], done, shared, arrived)
            else:
                done, shared, arrived = tie(done, shared, arrived)
            dense = [lax.psum_scatter(item, "dp", scatter_dimension=0, tiled=True) for item in shared[2:]]
        else:
            arrived = (up, down) if step < half else (up,)
        if step == half:
            done, dense = tie(done, dense)
        part_x[(0 if step == 1 else 1 - step)] = done
    run_experts(half, arrived)
    shared_branch, grad_shared = shared[:2]
    saved_x, saved_dy, saved_a, saved_dg, saved_du = [
        item.reshape(local, ep * capacity, item.shape[-1]) for item in buffers[0]
    ]

    def by_rows(left, right):
        return jnp.einsum("ecd,ecf->edf", left, right, preferred_element_type=f32).astype(bf16)

    came, expert_grads = None, []
    for step in range(1, half + 1):
        came = ring.scatter_step(part_x, came, step)
        if step <= 3:
            left, right = ((saved_x, saved_dg), (saved_x, saved_du), (saved_dy, saved_a))[step - 1]
            item = by_rows(left, right)
            came, item = tie(came, item)
            if step < 3:
                item = lax.psum_scatter(item, "dp", scatter_dimension=1, tiled=True)
            expert_grads.append(item)
    came, expert_grads[0] = tie(came, expert_grads[0])
    grad_routed = ring.scatter_end(part_x, came)
    grad_hidden_two = grad_shared + grad_routed
    grad_gain_two = jnp.sum(grad_hidden_two * normed_two, axis=0)
    scaled = grad_hidden_two * gain_two
    grad_out = grad_low.astype(f32)
    grad_middle = grad_out + inverse_two * (
        scaled - normed_two * jnp.mean(scaled * normed_two, axis=-1, keepdims=True)
    )
    grad_branch = grad_middle.astype(bf16)
    grad_attended = dot_nt(grad_branch, full_out).astype(bf16)

    by_head = grad_attended.reshape(rows, HEADS, HEAD).transpose(1, 0, 2)
    heads_out = jnp.concatenate(
        [by_head[:MAIN].reshape(ep, main_rows, HEAD), by_head[MAIN:].reshape(ep, side_rows, HEAD)], axis=1
    )
    part_y[half], grad_routed = tie(part_y[half], grad_routed)
    came_y = ring.scatter_step(part_y, None, 1)
    heads_out, attended_low, grad_branch, grad_gain_two = tie(heads_out, attended_low, grad_branch, grad_gain_two)
    head_grads = lax.all_to_all(heads_out, "ep", 0, 0, tiled=True)
    grad_full_out = dot_tn(attended_low, grad_branch).astype(bf16)

    gain_high = grad_gain_two.astype(bf16)
    gain_rest = (grad_gain_two - gain_high.astype(f32)).astype(bf16)
    gain_columns = dot_tn(jnp.stack([gain_high, gain_rest]), jnp.eye(2, HEAD, dtype=bf16))
    head_grads, came_y, grad_full_out, expert_grads[1] = tie(head_grads, came_y, grad_full_out, expert_grads[1])
    dense.append(lax.psum_scatter(grad_full_out, "dp", scatter_dimension=0, tiled=True))
    for step in range(2, half - 1):
        came_y = ring.scatter_step(part_y, came_y, step)
    grad_side = attention_backward(
        own, qkv, head_grads, attended, lse, cosine, sine, ep, rows, side_rows, 1, main_rows
    )
    grad_side, came_y, qkv, dense = tie(grad_side, came_y, qkv, dense)
    dense = lax.psum_scatter(jnp.concatenate(dense, axis=1), "ep", scatter_dimension=0, tiled=True).astype(f32)
    came_y = ring.scatter_step(part_y, came_y, half - 1)
    grad_main = attention_backward(
        own, qkv, head_grads, attended, lse, cosine, sine, ep, rows, main_rows, 0, 0
    )
    grad_main, grad_side, came_y, expert_grads[:2] = tie(grad_main, grad_side, came_y, expert_grads[:2])
    came_y = ring.scatter_step(part_y, came_y, half)

    part_h = {}
    for offset in range(-half + 1, half + 1):
        first = ring.member(offset) * rows
        part_h[offset] = (
            dot_nt(lax.dynamic_slice_in_dim(grad_main, first, rows, 0), w_cat[:, : 3 * HEAD])
            + dot_nt(lax.dynamic_slice_in_dim(grad_side, first, rows, 0), w_cat[:, 3 * HEAD :])
        ).astype(bf16)
    came = None
    inverse_one = lax.rsqrt(jnp.mean(residual * residual, axis=-1, keepdims=True) + epsilon)
    for step in range(1, half + 1):
        came = ring.scatter_step(part_h, came, step)
        if step == 1:
            next_parts = [part_h[offset] for offset in (half - 1, 1 - half)]
            came, next_parts, hidden_all = tie(came, next_parts, hidden_all)
            part_h[half - 1], part_h[1 - half] = next_parts
            head_sums = [dot_tn(hidden_all, grad_main), dot_tn(hidden_all, grad_side), gain_columns]
            head_sums = jnp.concatenate(head_sums, axis=1).astype(bf16)
            came_y, head_sums = tie(came_y, head_sums)
            head_sums = lax.psum_scatter(head_sums, "dp", scatter_dimension=0, tiled=True)
        if step == 2:
            early = [item.astype(f32) for item in expert_grads[:2]]
            came, came_y, part_h, expert_grads[:2], inverse_one = tie(came, came_y, part_h, early, inverse_one)
        if step == 3:
            came, head_sums, dense, last = tie(came, head_sums, dense, expert_grads[2])
            head_sums = lax.all_to_all(head_sums.reshape(ep, shard, 7 * HEAD), "ep", 0, 0, tiled=True)
            expert_grads[2] = lax.psum_scatter(last, "dp", scatter_dimension=1, tiled=True)
    head_sums = head_sums.astype(f32)
    grad_hidden_one = ring.scatter_end(part_h, came)
    output = (middle + shared_branch + ring.scatter_end(part_y, came_y)).astype(bf16)
    main_sums = head_sums[:, :, : 3 * HEAD].reshape(MAIN, copies, shard, 3, HEAD).sum(1)
    gain_sums = head_sums[:, :, 6 * HEAD] + head_sums[:, :, 6 * HEAD + 1]
    side_sums = head_sums[:, :, 3 * HEAD : 6 * HEAD].reshape(HEADS - MAIN, sharers * copies, shard, 3, HEAD).sum(1)
    head_sums = jnp.concatenate([main_sums, side_sums], axis=0)
    projections = [head_sums[:, :, i].transpose(1, 0, 2).reshape(shard, width) for i in range(3)]
    grad_gain_one = sum(
        jnp.sum(w.astype(f32) * g, axis=1) for w, g in zip((w_query, w_key, w_value), projections)
    ) / norm1_gain.astype(f32)

    normed_one = residual * inverse_one
    scaled = grad_hidden_one * gain_one
    grad_input = grad_middle + inverse_one * (
        scaled - normed_one * jnp.mean(scaled * normed_one, axis=-1, keepdims=True)
    )
    return (
        output[None],
        grad_input[None],
        grad_gain_one,
        gain_sums.sum(0),
        projections[0],
        projections[1],
        projections[2],
        dense[:, 3 * inner : 3 * inner + width],
        dense[:, :inner],
        dense[:, inner : 2 * inner],
        dense[:, 2 * inner : 3 * inner].T,
        expert_grads[0],
        expert_grads[1],
        expert_grads[2].astype(f32).transpose(0, 2, 1),
    )


def solution(mesh):
    by_token = P("dp", "ep", None)
    by_row = P(("dp", "ep"), None)
    in_specs = (
        (by_token,) * 5
        + (P(("dp", "ep")),) * 2
        + (by_row,) * 6
        + (P(None, ("dp", "ep")),)
        + (P("ep", None, None),) * 3
    )
    out_specs = (
        (by_token,) * 2
        + (P(("dp", "ep")),) * 2
        + (by_row,) * 6
        + (P(None, ("dp", "ep")), P("ep", "dp", None), P("ep", "dp", None), P("ep", None, "dp"))
    )
    return jax.shard_map(shards, mesh=mesh, in_specs=in_specs, out_specs=out_specs, check_vma=False)
```

```python
import math

import jax
import jax.numpy as jnp
from jax import lax
from jax.experimental import pallas as pl
from jax.experimental.pallas import tpu as pltpu
from jax.sharding import PartitionSpec as P

HEADS = 10
HEAD = 128
MAIN = 8
epsilon = 1e-06
negative = -1e30
bf16 = jnp.bfloat16
f32 = jnp.float32
VMEM_LIMIT = 64 * 1024 * 1024 - 128 * 1024


def dot(a, b):
    return jnp.dot(a, b, preferred_element_type=f32)


def dot_nt(a, b):
    return lax.dot_general(a, b, (((1,), (1,)), ((), ())), preferred_element_type=f32)


def dot_tn(a, b):
    return lax.dot_general(a, b, (((0,), (0,)), ((), ())), preferred_element_type=f32)


def tie(*values):
    return lax.optimization_barrier(values)


def after(value, *others):
    return lax.optimization_barrier((value, others))[0]


def cycle_of(size):
    if size == 16:
        return [0, 1, 2, 3, 7, 6, 5, 9, 10, 11, 15, 14, 13, 12, 8, 4]
    return list(range(0, size, 2)) + list(range(size - 1, 0, -2))


def spec(shape, index, single=False):
    if single:
        return pl.BlockSpec(shape, index, pipeline_mode=pl.Buffered(1))
    return pl.BlockSpec(shape, index)


class Ring:
    def __init__(self, size):
        self.size = size
        self.half = size // 2
        self.order = cycle_of(size)
        place = [0] * size
        for at, member in enumerate(self.order):
            place[member] = at
        self.forward = [(self.order[i], self.order[(i + 1) % size]) for i in range(size)]
        self.backward = [(self.order[i], self.order[(i - 1) % size]) for i in range(size)]
        table = [[self.order[(place[me] + offset) % size] for offset in range(size)] for me in range(size)]
        self.members = lax.dynamic_index_in_dim(jnp.array(table, jnp.int32), lax.axis_index("ep"), 0, keepdims=False)

    def member(self, offset):
        return self.members[offset % self.size]

    def step(self, up, down, number):
        if number == self.half:
            cut = up.shape[0] // 2
            up, down = up[:cut], down[cut:]
        return lax.ppermute(up, "ep", self.forward), lax.ppermute(down, "ep", self.backward)

    def gather(self, own, visit):
        up, down, arrived, done = own, own, (own,), None
        for step in range(1, self.half + 1):
            if done is not None:
                up, down, done = lax.optimization_barrier((up, down, done))
            up, down = self.step(up, down, step)
            done = visit(step - 1, arrived)
            arrived = (up, down)
        visit(self.half, arrived)

    def scatter_step(self, parts, came, number):
        cut = parts[0].shape[0] // 2
        away = self.half - number + 1
        if number == 1:
            up, down = parts[away][:cut], parts[away][cut:]
        else:
            ahead, behind = parts[away], parts[-away]
            up, down = came
            if number == 2:
                up = jnp.concatenate([(ahead[:cut].astype(f32) + up.astype(f32)).astype(bf16), ahead[cut:]], axis=0)
                down = jnp.concatenate([behind[:cut], (behind[cut:].astype(f32) + down.astype(f32)).astype(bf16)], axis=0)
            else:
                up = (ahead.astype(f32) + up.astype(f32)).astype(bf16)
                down = (behind.astype(f32) + down.astype(f32)).astype(bf16)
        return lax.ppermute(up, "ep", self.forward), lax.ppermute(down, "ep", self.backward)

    def scatter_end(self, parts, came):
        return parts[0].astype(f32) + came[0].astype(f32) + came[1].astype(f32)


def qkv_kernel(members_ref, tok_ref, gain_ref, w_ref, cos_ref, sin_ref, *rest):
    hid_ref, qkv_ref = rest[-2:]
    x = tok_ref[...].astype(f32)
    inverse = lax.rsqrt(jnp.mean(x * x, axis=-1, keepdims=True) + epsilon)
    hidden = (x * inverse * gain_ref[...]).astype(bf16)
    hid_ref[...] = hidden
    out = dot(hidden, w_ref[...])
    cosine, sine = cos_ref[...], sin_ref[...]
    for slot in range(6):
        u = out[:, slot * HEAD : (slot + 1) * HEAD]
        if slot % 3 != 2:
            u = u * cosine + pltpu.roll(u, HEAD // 2, 1) * sine
        qkv_ref[:, slot * HEAD : (slot + 1) * HEAD] = u.astype(bf16)


def qkv_piece(members, offset, shift, piece, tile, gain, w_cat, cosine, sine, buffers):
    rows, width = piece.shape
    length = cosine.shape[0]
    cols = w_cat.shape[1]
    aliased = () if buffers is None else tuple(buffers)
    n_in = 6
    at = lambda i, m: (2 * m[offset] + shift + i, 0)
    return pl.pallas_call(
        qkv_kernel,
        out_shape=(jax.ShapeDtypeStruct((length, width), bf16), jax.ShapeDtypeStruct((length, cols), bf16)),
        grid_spec=pltpu.PrefetchScalarGridSpec(
            num_scalar_prefetch=1,
            grid=(rows // tile,),
            in_specs=[
                pl.BlockSpec((tile, width), lambda i, b: (i, 0)),
                pl.BlockSpec((1, width), lambda i, b: (0, 0)),
                pl.BlockSpec((width, cols), lambda i, b: (0, 0)),
                pl.BlockSpec((tile, HEAD), at),
                pl.BlockSpec((tile, HEAD), at),
            ]
            + [pl.BlockSpec(memory_space=pl.ANY)] * len(aliased),
            out_specs=[
                pl.BlockSpec((tile, width), at),
                pl.BlockSpec((tile, cols), at),
            ],
        ),
        input_output_aliases={n_in + i: i for i in range(len(aliased))},
        compiler_params=pltpu.CompilerParams(vmem_limit_bytes=32 * 1024 * 1024),
        cost_estimate=pl.CostEstimate(
            flops=2 * rows * width * cols, bytes_accessed=4 * rows * width + 2 * (rows + width) * cols, transcendentals=0
        ),
        name="norm_project_rotate",
    )(members, piece, gain, w_cat, cosine, sine, *aliased)


def attention_forward(own, qkv, blocks, rows, main_rows, side_rows):
    scale = math.log2(math.e) / math.sqrt(HEAD)
    length = qkv.shape[0]
    tall = main_rows + side_rows

    def kernel(own_ref, qkv_ref, low_ref, att_ref, lse_ref):
        block = pl.program_id(0)

        def piece(col, offset, count):
            first = pl.multiple_of(block * rows + offset, 32)
            return qkv_ref[pl.ds(first, count), col : col + HEAD]

        offsets = (own_ref[0], own_ref[1])
        counts = (main_rows, side_rows)
        queries = [piece(3 * HEAD * i, offsets[i], counts[i]) for i in range(2)]

        def step(i, at, state, diagonal):
            best, total, acc = state
            first = pl.multiple_of(at * rows, rows)
            col = 3 * HEAD * i
            keys = qkv_ref[pl.ds(first, rows), col + HEAD : col + 2 * HEAD]
            values = qkv_ref[pl.ds(first, rows), col + 2 * HEAD : col + 3 * HEAD]
            scores = dot_nt(queries[i], keys) * scale
            if diagonal:
                q_at = lax.broadcasted_iota(jnp.int32, scores.shape, 0) + offsets[i]
                k_at = lax.broadcasted_iota(jnp.int32, scores.shape, 1)
                scores = jnp.where(q_at >= k_at, scores, negative)
            top = jnp.maximum(best, jnp.max(scores, axis=1, keepdims=True))
            weights = jnp.exp2(scores - top)
            factor = jnp.exp2(best - top)
            total = total * factor + jnp.sum(weights, axis=1, keepdims=True)
            acc = acc * factor + dot(weights.astype(bf16), values)
            return top, total, acc

        def both(at, states, diagonal=False):
            return tuple(step(i, at, states[i], diagonal) for i in range(2))

        start = tuple(
            (jnp.full((c, 1), negative, f32), jnp.zeros((c, 1), f32), jnp.zeros((c, HEAD), f32)) for c in counts
        )
        states = lax.fori_loop(0, block, both, start)
        states = both(block, states, True)
        at = 0
        for i in range(2):
            best, total, acc = states[i]
            attended = acc / total
            low_ref[0, at : at + counts[i]] = attended.astype(bf16)
            att_ref[0, at : at + counts[i]] = attended
            lse = jnp.broadcast_to(best + jnp.log2(total), (counts[i], HEAD))
            lse_ref[0, :, at : at + counts[i]] = jnp.transpose(lse)[0:8]
            at += counts[i]

    return pl.pallas_call(
        kernel,
        out_shape=(
            jax.ShapeDtypeStruct((blocks, tall, HEAD), bf16),
            jax.ShapeDtypeStruct((blocks, tall, HEAD), f32),
            jax.ShapeDtypeStruct((blocks, 8, tall), f32),
        ),
        grid_spec=pltpu.PrefetchScalarGridSpec(
            num_scalar_prefetch=1,
            grid=(blocks,),
            in_specs=[spec((length, qkv.shape[1]), lambda s, o: (0, 0), True)],
            out_specs=[
                pl.BlockSpec((1, tall, HEAD), lambda s, o: (s, 0, 0)),
                pl.BlockSpec((1, tall, HEAD), lambda s, o: (s, 0, 0)),
                pl.BlockSpec((1, 8, tall), lambda s, o: (s, 0, 0)),
            ],
        ),
        compiler_params=pltpu.CompilerParams(vmem_limit_bytes=48 * 1024 * 1024),
        cost_estimate=pl.CostEstimate(
            flops=4 * length * tall * blocks * HEAD // 2, bytes_accessed=16 * length * HEAD, transcendentals=length * tall * blocks // 2
        ),
        name="attention_forward",
    )(own, qkv)


def attention_backward(own, qkv, grads, attended, lse, cosine, sine, blocks, rows, count, slot, start, buffer=None):
    scale = 1.0 / math.sqrt(HEAD)
    scale_two = math.log2(math.e) * scale
    length = qkv.shape[0]
    tall = grads.shape[1]
    cols = 3 * HEAD
    here = slice(start, start + count)

    def kernel(own_ref, qkv_ref, grad_ref, att_ref, lse_ref, cos_ref, sin_ref, *rest):
        out_ref, key_sum, value_sum = rest[-3:]
        block = pl.program_id(0)
        offset = own_ref[slot]

        @pl.when(block == 0)
        def _():
            key_sum[...] = jnp.zeros_like(key_sum)
            value_sum[...] = jnp.zeros_like(value_sum)
            if count < rows:
                out_ref[:, :HEAD] = jnp.zeros((length, HEAD), bf16)

        mine = pl.multiple_of(block * rows + offset, 32)
        queries = qkv_ref[pl.ds(mine, count), :HEAD]
        grad = grad_ref[0, here]
        lse_row = lse_ref[0, 0:1, here]
        product = grad.astype(f32) * att_ref[0, here]
        delta = jnp.sum(jnp.transpose(product), axis=0, keepdims=True)

        def step(at, dq, diagonal=False):
            first = pl.multiple_of(at * rows, rows)
            keys = qkv_ref[pl.ds(first, rows), HEAD : 2 * HEAD]
            values = qkv_ref[pl.ds(first, rows), 2 * HEAD :]
            scores = dot_nt(keys, queries) * scale_two
            if diagonal:
                k_at = lax.broadcasted_iota(jnp.int32, scores.shape, 0)
                q_at = lax.broadcasted_iota(jnp.int32, scores.shape, 1) + offset
                scores = jnp.where(q_at >= k_at, scores, negative)
            probs = jnp.exp2(scores - lse_row)
            grad_probs = dot_nt(values, grad)
            grad_scores = (probs * (grad_probs - delta)).astype(bf16)
            value_sum[pl.ds(first, rows)] += dot(probs.astype(bf16), grad)
            key_sum[pl.ds(first, rows)] += dot(grad_scores, queries)
            return dq + dot_tn(grad_scores, keys)

        dq = step(block, lax.fori_loop(0, block, step, jnp.zeros((count, HEAD), f32)), True)

        def turn_back(value, first, size):
            cosine_part = cos_ref[pl.ds(first, size)]
            sine_part = sin_ref[pl.ds(first, size)]
            value = value * scale
            return (value * cosine_part - pltpu.roll(value, HEAD // 2, 1) * sine_part).astype(bf16)

        out_ref[pl.ds(mine, count), :HEAD] = turn_back(dq, mine, count)

        @pl.when(block == blocks - 1)
        def _():
            def finish(at, carry):
                first = pl.multiple_of(at * rows, rows)
                out_ref[pl.ds(first, rows), HEAD : 2 * HEAD] = turn_back(key_sum[pl.ds(first, rows)], first, rows)
                out_ref[pl.ds(first, rows), 2 * HEAD :] = value_sum[pl.ds(first, rows)].astype(bf16)
                return carry

            lax.fori_loop(0, blocks, finish, 0)

    aliased = () if buffer is None else (buffer,)
    return pl.pallas_call(
        kernel,
        out_shape=jax.ShapeDtypeStruct((length, 2 * cols), bf16),
        grid_spec=pltpu.PrefetchScalarGridSpec(
            num_scalar_prefetch=1,
            grid=(blocks,),
            in_specs=[
                spec((length, cols), lambda s, o: (0, slot), True),
                pl.BlockSpec((1, tall, HEAD), lambda s, o: (s, 0, 0)),
                pl.BlockSpec((1, tall, HEAD), lambda s, o: (s, 0, 0)),
                pl.BlockSpec((1, 8, tall), lambda s, o: (s, 0, 0)),
                spec((length, HEAD), lambda s, o: (0, 0), True),
                spec((length, HEAD), lambda s, o: (0, 0), True),
            ]
            + [pl.BlockSpec(memory_space=pl.ANY)] * len(aliased),
            out_specs=spec((length, cols), lambda s, o: (0, slot), True),
            scratch_shapes=[pltpu.VMEM((length, HEAD), f32)] * 2,
        ),
        input_output_aliases={7 + i: i for i in range(len(aliased))},
        compiler_params=pltpu.CompilerParams(vmem_limit_bytes=40 * 1024 * 1024),
        cost_estimate=pl.CostEstimate(
            flops=10 * length * count * blocks * HEAD // 2, bytes_accessed=20 * length * HEAD, transcendentals=length * count * blocks // 2
        ),
        name="attention_backward",
    )(own, qkv, grads, attended, lse, cosine, sine, *aliased)


def expert_call(members, offsets, hidden, grads, rank_row, rank_col, route, w_gate, w_up, w_down, capacity, first, total, buffers):
    count = len(hidden)
    rows, width = hidden[0].shape
    local, _, inner = w_gate.shape
    aliased = () if buffers is None else tuple(buffers)
    widths = (width, width, inner, inner, inner)

    def kernel(members_ref, *refs):
        h_refs, z_refs, row_refs, col_refs, gate_refs = (refs[i * count : (i + 1) * count] for i in range(5))
        wg_ref, wu_ref, wd_ref = refs[5 * count : 5 * count + 3]
        rest = refs[5 * count + 3 + len(aliased) :]
        outs_y, outs_x = rest[:count], rest[count : 2 * count]
        x_ref, dy_ref, a_ref, dg_ref, du_ref, keep_y, keep_x = rest[2 * count :]
        expert = pl.program_id(0)
        for p in range(count):
            slots = lax.broadcasted_iota(jnp.int32, (capacity, rows), 0).astype(f32)
            hit = slots == row_refs[p][0, expert]
            pick = jnp.where(hit, 1.0, 0.0).astype(bf16)
            gate = jnp.sum(jnp.where(hit, gate_refs[p][0, expert], 0.0), axis=1, keepdims=True)
            x = dot(pick, h_refs[p][...]).astype(bf16)
            dy = (dot(pick, z_refs[p][...]) * gate).astype(bf16)
            x_ref[0, p] = x
            dy_ref[0, p] = dy
            g = dot(x, wg_ref[0])
            u = dot(x, wu_ref[0])
            sigma = 1.0 / (1.0 + jnp.exp(-g))
            act = g * sigma
            a = (act * u).astype(bf16)
            a_ref[0, p] = a
            da = dot_nt(dy, wd_ref[0])
            du = (da * act).astype(bf16)
            dg = (da * u * sigma * (1.0 + g * (1.0 - sigma))).astype(bf16)
            du_ref[0, p] = du
            dg_ref[0, p] = dg
            y = dot(a, wd_ref[0]).astype(bf16)
            at = pl.multiple_of(expert * capacity, 16)
            keep_y[p, pl.ds(at, capacity)] = (y.astype(f32) * gate).astype(bf16)
            dx = dot_nt(dg, wg_ref[0]) + dot_nt(du, wu_ref[0])
            keep_x[p, pl.ds(at, capacity)] = dx.astype(bf16)

        @pl.when(expert == local - 1)
        def _():
            for p in range(count):
                slots = lax.broadcasted_iota(jnp.int32, (rows, capacity), 1).astype(f32)
                place = jnp.concatenate(
                    [jnp.where(slots == col_refs[p][0, e], 1.0, 0.0).astype(bf16) for e in range(local)], axis=1
                )
                outs_y[p][...] = dot(place, keep_y[p]).astype(bf16)
                outs_x[p][...] = dot(place, keep_x[p]).astype(bf16)

    piece = jax.ShapeDtypeStruct((rows, width), bf16)
    by_expert = lambda e, s: (e, 0, 0)
    slot = lambda e, s: (e, first // count, 0, 0)

    def of_source(shape):
        zeros = (0,) * (len(shape) - 1)
        return [pl.BlockSpec(shape, lambda e, s, p=p: (s[offsets[p]],) + zeros, pipeline_mode=pl.Buffered(1)) for p in range(count)]

    return pl.pallas_call(
        kernel,
        out_shape=[piece] * (2 * count) + [jax.ShapeDtypeStruct((local, total, capacity, w), bf16) for w in widths],
        grid_spec=pltpu.PrefetchScalarGridSpec(
            num_scalar_prefetch=1,
            grid=(local,),
            in_specs=[spec((rows, width), lambda e, s: (0, 0), True)] * (2 * count)
            + of_source((1, local, 1, rows))
            + of_source((1, local, rows, 1))
            + of_source((1, local, 1, rows))
            + [
                pl.BlockSpec((1, width, inner), by_expert),
                pl.BlockSpec((1, width, inner), by_expert),
                pl.BlockSpec((1, inner, width), by_expert),
            ]
            + [pl.BlockSpec(memory_space=pl.ANY)] * len(aliased),
            out_specs=[spec((rows, width), lambda e, s: (0, 0), True)] * (2 * count)
            + [pl.BlockSpec((1, count, capacity, w), slot) for w in widths],
            scratch_shapes=[pltpu.VMEM((count, local * capacity, width), bf16)] * 2,
        ),
        input_output_aliases={1 + 5 * count + 3 + i: 2 * count + i for i in range(len(aliased))},
        compiler_params=pltpu.CompilerParams(vmem_limit_bytes=VMEM_LIMIT),
        cost_estimate=pl.CostEstimate(
            flops=count * 2 * local * capacity * width * (6 * inner + 4 * rows),
            bytes_accessed=2 * local * (3 * width * inner + count * capacity * (2 * width + 3 * inner)) + count * 8 * rows * width,
            transcendentals=count * local * capacity * inner,
        ),
        name="experts",
    )(
        members,
        *hidden,
        *grads,
        *[rank_row] * count,
        *[rank_col] * count,
        *[route] * count,
        w_gate,
        w_up,
        w_down,
        *aliased,
    )


def shared_expert(hidden, grads, weights, inner):
    rows, width = hidden.shape
    tile = rows // 2

    def kernel(h_ref, z_ref, wg_ref, wu_ref, wd_ref, branch_ref, back_ref, act_ref, pre_ref):
        gate_pre = dot(h_ref[...], wg_ref[...])
        up_pre = dot(h_ref[...], wu_ref[...])
        grad_act = dot(z_ref[...], wd_ref[...])
        sigma = 1.0 / (1.0 + jnp.exp(-gate_pre))
        act = gate_pre * sigma
        low = (act * up_pre).astype(bf16)
        act_ref[...] = low
        grad_up = (grad_act * act).astype(bf16)
        grad_gate = (grad_act * up_pre * sigma * (1.0 + gate_pre * (1.0 - sigma))).astype(bf16)
        pre_ref[:, :inner] = grad_gate
        pre_ref[:, inner:] = grad_up
        branch_ref[...] = dot_nt(low, wd_ref[...])
        back_ref[...] = dot_nt(grad_gate, wg_ref[...]) + dot_nt(grad_up, wu_ref[...])

    by_row = lambda i: (i, 0)
    return pl.pallas_call(
        kernel,
        grid=(rows // tile,),
        out_shape=(
            jax.ShapeDtypeStruct((rows, width), f32),
            jax.ShapeDtypeStruct((rows, width), f32),
            jax.ShapeDtypeStruct((rows, inner), bf16),
            jax.ShapeDtypeStruct((rows, 2 * inner), bf16),
        ),
        in_specs=[pl.BlockSpec((tile, width), by_row)] * 2
        + [pl.BlockSpec((width, inner), lambda i, n=n: (0, n), pipeline_mode=pl.Buffered(1)) for n in range(3)],
        out_specs=[
            pl.BlockSpec((tile, width), by_row),
            pl.BlockSpec((tile, width), by_row),
            pl.BlockSpec((tile, inner), by_row),
            pl.BlockSpec((tile, 2 * inner), by_row),
        ],
        compiler_params=pltpu.CompilerParams(vmem_limit_bytes=40 * 1024 * 1024),
        cost_estimate=pl.CostEstimate(
            flops=12 * rows * width * inner, bytes_accessed=12 * rows * width + 6 * width * inner, transcendentals=rows * inner
        ),
        name="shared_expert",
    )(hidden, grads, weights, weights, weights)


def shards(
    tokens, cotangent, expert_ids, keep, gates, norm1_gain, norm2_gain, w_query, w_key, w_value, w_out,
    shared_gate, shared_up, shared_down, expert_gate, expert_up, expert_down,
):
    ep = lax.axis_size("ep")
    me = lax.axis_index("ep")
    ring = Ring(ep)
    half = ring.half
    token_rows = tokens[0]
    grad_low = cotangent[0]
    rows, width = token_rows.shape
    length = rows * ep
    local = expert_gate.shape[0]
    inner = expert_gate.shape[2]
    experts = local * ep
    shard = w_query.shape[0]
    copies = ep // MAIN
    sharers = MAIN // (HEADS - MAIN)
    main_rows = rows // copies
    side_rows = rows // (sharers * copies)
    tall = main_rows + side_rows
    capacity = min(rows, rows * 10 // experts)
    main_part = me % copies
    side_part = ((me // copies) % sharers) * copies + main_part
    own = jnp.stack([main_part * main_rows, side_part * side_rows]).astype(jnp.int32)

    gains = jnp.concatenate([norm1_gain[:, None], norm2_gain[:, None], jnp.zeros((shard, HEAD - 2), bf16)], axis=1)
    messages = []
    for member in range(ep):
        main_head = member // copies
        side_head = MAIN + main_head // sharers
        messages.append(
            jnp.concatenate(
                [
                    weight[:, head * HEAD : (head + 1) * HEAD]
                    for head in (main_head, side_head)
                    for weight in (w_query, w_key, w_value)
                ]
                + [gains],
                axis=1,
            )
        )
    head_rows = lax.all_to_all(jnp.stack(messages), "ep", 0, 0, tiled=True)

    chosen = expert_ids[0][:, :, None] == jnp.arange(experts, dtype=jnp.int32)[None, None, :]
    weight_here = gates[0] * keep[0].astype(f32)
    route = jnp.sum(jnp.where(chosen, weight_here[:, :, None], 0.0), axis=1)
    route = lax.all_to_all(route.T.reshape(ep, local, rows), "ep", 0, 0, tiled=True)
    used = route > 0.0
    before = (jnp.arange(rows)[:, None] < jnp.arange(rows)[None, :]).astype(bf16)
    rank = dot(used.astype(bf16).reshape(ep * local, rows), before).reshape(ep, local, rows)
    rank = jnp.where(used, rank, -1.0)

    freqs = jnp.exp(jnp.arange(HEAD // 2, dtype=f32) * (-2.0 * math.log(10000.0) / HEAD))
    turned = jnp.arange(length, dtype=jnp.int32).astype(f32)[:, None] * freqs[None, :]
    cosine, sine = jnp.cos(turned), jnp.sin(turned)
    cosine = jnp.concatenate([cosine, cosine], axis=1)
    sine = jnp.concatenate([-sine, sine], axis=1)

    tile = rows // 2
    arrivals, known = [], {}

    def project(steps):
        for step in steps:
            for i, part in enumerate(arrivals[step]):
                offset = 0 if step == 0 else (half if step == half else (-step, step)[i])
                known["buffers"] = qkv_piece(
                    ring.members, offset % ep, i if step == half else 0, part, tile, known["gains"][0], known["w_cat"],
                    cosine, sine, known.get("buffers"),
                )

    up, down = token_rows, token_rows
    arrivals.append((token_rows,))
    for step in range(1, half + 1):
        up, down = ring.step(up, down, step)
        if step == 1:
            head_rows, up, down = tie(head_rows, up, down)
            head_weights = lax.all_gather(head_rows.reshape(ep * shard, 7 * HEAD), "dp", axis=0, tiled=True)
            gain_rows = head_weights[:, 6 * HEAD : 6 * HEAD + 2].astype(f32).T
            gain_one, gain_two = gain_rows[0:1], gain_rows[1:2]
            w_cat = head_weights[:, : 6 * HEAD]
            known["gains"], known["w_cat"] = (gain_one, gain_two), w_cat
        if step == 2:
            route, rank, up, down = tie(route, rank, up, down)
        if step == half - 1:
            project(range(half - 1))
            packed = jnp.concatenate([w_out, shared_gate, shared_up, shared_down.T], axis=1)
            up, down, packed, known["buffers"] = tie(up, down, packed, known["buffers"])
            packed = lax.all_gather(packed, "ep", axis=0, tiled=True)
        arrivals.append((up, down))
    project([half - 1, half])
    hidden_all, qkv = known["buffers"]

    grad_pieces = {0: (grad_low,)}
    grad_low, qkv = tie(grad_low, qkv)
    grad_pieces[1] = ring.step(grad_low, grad_low, 1)

    low, attended, lse = attention_forward(own, qkv, ep, rows, main_rows, side_rows)
    low, grad_pieces[1], packed = tie(low, grad_pieces[1], packed)
    full_out = lax.all_gather(packed[:, :width], "dp", axis=0, tiled=True)
    grad_pieces[2] = ring.step(*grad_pieces[1], 2)
    heads_in = lax.all_to_all(low, "ep", 0, 0, tiled=True)
    rank_row, rank_col, route_row = rank[:, :, None, :], rank[:, :, :, None], route[:, :, None, :]
    heads_in, rank_col = tie(heads_in, rank_col)
    main_in = heads_in[:, :main_rows].reshape(MAIN, rows, HEAD)
    side_in = heads_in[:, main_rows:].reshape(HEADS - MAIN, rows, HEAD)
    attended_low = jnp.concatenate([main_in, side_in], axis=0).transpose(1, 0, 2).reshape(rows, width)

    residual = token_rows.astype(f32)
    middle = residual + dot(attended_low, full_out)
    inverse_two = lax.rsqrt(jnp.mean(middle * middle, axis=-1, keepdims=True) + epsilon)
    normed_two = middle * inverse_two
    hidden_two = (normed_two * gain_two).astype(bf16)

    hidden_two, grad_pieces[2], packed = tie(hidden_two, grad_pieces[2], packed)
    packed = lax.all_gather(packed[:, width:], "dp", axis=0, tiled=True)
    part_y, part_x, buffers = {}, {}, [None]

    def run_experts(step, arrived):
        grads = grad_pieces[step]
        if step == half:
            group, first = (half,), ep - 1
        elif step == 0:
            group, first = (0,), ep - 2
        else:
            group, first = (-step, step), 2 * (step - 1)
        outs = expert_call(
            ring.members,
            [offset % ep for offset in group],
            arrived,
            grads,
            rank_row,
            rank_col,
            route_row,
            expert_gate,
            expert_up,
            expert_down,
            capacity,
            first,
            ep,
            buffers[0],
        )
        for i, offset in enumerate(group):
            part_y[offset] = outs[i]
            part_x[offset] = outs[len(group) + i]
        buffers[0] = outs[2 * len(group) :]
        return outs[len(group)]

    def run_shared(hidden, grads):
        branch, back, act, grad_pre = shared_expert(hidden, grads, packed, inner)
        return branch, back, dot_tn(hidden, grad_pre).astype(bf16), dot_tn(grads, act).astype(bf16)

    up, down, arrived = hidden_two, hidden_two, (hidden_two,)
    for step in range(1, half + 1):
        if step < half:
            up, down = ring.step(up, down, step)
            if step >= 4:
                grad_pieces[step] = ring.step(*grad_pieces[step - 1], step)
        else:
            up = lax.ppermute(up, "ep", ring.forward)
            grad_pieces[step] = (lax.ppermute(grad_pieces[step - 1][1], "ep", ring.backward),)
        done = run_experts(step - 1, arrived)
        up, down, done, grad_pieces[step] = tie(up, down, done, grad_pieces[step])
        if step == 2:
            hidden_two, grad_low, done = tie(hidden_two, grad_low, done)
            shared = run_shared(hidden_two, grad_low)
            arrived = (up, down)
            if half > 3:
                grad_pieces[3] = ring.step(*grad_pieces[2], 3)
                grad_pieces[3], done, shared, arrived = tie(grad_pieces[3], done, shared, arrived)
            else:
                done, shared, arrived = tie(done, shared, arrived)
            dense = [lax.psum_scatter(item, "dp", scatter_dimension=0, tiled=True) for item in shared[2:]]
        else:
            arrived = (up, down) if step < half else (up,)
        if step == half:
            done, dense = tie(done, dense)
        part_x[(0 if step == 1 else 1 - step)] = done
    run_experts(half, arrived)
    shared_branch, grad_shared = shared[:2]
    saved_x, saved_dy, saved_a, saved_dg, saved_du = [
        item.reshape(local, ep * capacity, item.shape[-1]) for item in buffers[0]
    ]

    def by_rows(left, right):
        return jnp.einsum("ecd,ecf->edf", left, right, preferred_element_type=f32).astype(bf16)

    came, expert_grads = None, []
    for step in range(1, half + 1):
        came = ring.scatter_step(part_x, came, step)
        if step <= 3:
            left, right = ((saved_x, saved_dg), (saved_x, saved_du), (saved_dy, saved_a))[step - 1]
            item = by_rows(left, right)
            came, item = tie(came, item)
            if step < 3:
                item = lax.psum_scatter(item, "dp", scatter_dimension=1, tiled=True)
            expert_grads.append(item)
    came, expert_grads[0] = tie(came, expert_grads[0])
    grad_routed = ring.scatter_end(part_x, came)
    grad_hidden_two = grad_shared + grad_routed
    grad_gain_two = jnp.sum(grad_hidden_two * normed_two, axis=0)
    scaled = grad_hidden_two * gain_two
    grad_out = grad_low.astype(f32)
    grad_middle = grad_out + inverse_two * (
        scaled - normed_two * jnp.mean(scaled * normed_two, axis=-1, keepdims=True)
    )
    grad_branch = grad_middle.astype(bf16)
    grad_attended = dot_nt(grad_branch, full_out).astype(bf16)

    by_head = grad_attended.reshape(rows, HEADS, HEAD).transpose(1, 0, 2)
    heads_out = jnp.concatenate(
        [by_head[:MAIN].reshape(ep, main_rows, HEAD), by_head[MAIN:].reshape(ep, side_rows, HEAD)], axis=1
    )
    part_y[half], grad_routed = tie(part_y[half], grad_routed)
    came_y = ring.scatter_step(part_y, None, 1)
    heads_out, attended_low, grad_branch, grad_gain_two = tie(heads_out, attended_low, grad_branch, grad_gain_two)
    head_grads = lax.all_to_all(heads_out, "ep", 0, 0, tiled=True)
    grad_full_out = dot_tn(attended_low, grad_branch).astype(bf16)

    gain_high = grad_gain_two.astype(bf16)
    gain_rest = (grad_gain_two - gain_high.astype(f32)).astype(bf16)
    gain_columns = dot_tn(jnp.stack([gain_high, gain_rest]), jnp.eye(2, HEAD, dtype=bf16))
    head_grads, came_y, grad_full_out, expert_grads[1] = tie(head_grads, came_y, grad_full_out, expert_grads[1])
    dense.append(lax.psum_scatter(grad_full_out, "dp", scatter_dimension=0, tiled=True))
    for step in range(2, half - 1):
        came_y = ring.scatter_step(part_y, came_y, step)
    grad_side = attention_backward(
        own, qkv, head_grads, attended, lse, cosine, sine, ep, rows, side_rows, 1, main_rows
    )
    grad_side, came_y, qkv, dense = tie(grad_side, came_y, qkv, dense)
    dense = lax.psum_scatter(jnp.concatenate(dense, axis=1), "ep", scatter_dimension=0, tiled=True).astype(f32)
    came_y = ring.scatter_step(part_y, came_y, half - 1)
    grad_main = attention_backward(
        own, qkv, head_grads, attended, lse, cosine, sine, ep, rows, main_rows, 0, 0, grad_side
    )
    grad_qkv, came_y, expert_grads[:2] = tie(grad_main, came_y, expert_grads[:2])
    came_y = ring.scatter_step(part_y, came_y, half)

    part_h = {}
    for offset in range(-half + 1, half + 1):
        block = lax.dynamic_slice_in_dim(grad_qkv, ring.member(offset) * rows, rows, 0)
        part_h[offset] = dot_nt(block, w_cat).astype(bf16)
    came = None
    inverse_one = lax.rsqrt(jnp.mean(residual * residual, axis=-1, keepdims=True) + epsilon)
    for step in range(1, half + 1):
        came = ring.scatter_step(part_h, came, step)
        if step == 1:
            next_parts = [part_h[offset] for offset in (half - 1, 1 - half)]
            came, next_parts, hidden_all = tie(came, next_parts, hidden_all)
            part_h[half - 1], part_h[1 - half] = next_parts
            head_sums = jnp.concatenate([dot_tn(hidden_all, grad_qkv), gain_columns], axis=1).astype(bf16)
            came_y, head_sums = tie(came_y, head_sums)
            head_sums = lax.psum_scatter(head_sums, "dp", scatter_dimension=0, tiled=True)
        if step == 2:
            early = [item.astype(f32) for item in expert_grads[:2]]
            came, came_y, part_h, expert_grads[:2], inverse_one = tie(came, came_y, part_h, early, inverse_one)
        if step == 3:
            came, head_sums, dense, last = tie(came, head_sums, dense, expert_grads[2])
            head_sums = lax.all_to_all(head_sums.reshape(ep, shard, 7 * HEAD), "ep", 0, 0, tiled=True)
            expert_grads[2] = lax.psum_scatter(last, "dp", scatter_dimension=1, tiled=True)
    head_sums = head_sums.astype(f32)
    grad_hidden_one = ring.scatter_end(part_h, came)
    output = (middle + shared_branch + ring.scatter_end(part_y, came_y)).astype(bf16)
    main_sums = head_sums[:, :, : 3 * HEAD].reshape(MAIN, copies, shard, 3, HEAD).sum(1)
    gain_sums = head_sums[:, :, 6 * HEAD] + head_sums[:, :, 6 * HEAD + 1]
    side_sums = head_sums[:, :, 3 * HEAD : 6 * HEAD].reshape(HEADS - MAIN, sharers * copies, shard, 3, HEAD).sum(1)
    head_sums = jnp.concatenate([main_sums, side_sums], axis=0)
    projections = [head_sums[:, :, i].transpose(1, 0, 2).reshape(shard, width) for i in range(3)]
    grad_gain_one = sum(
        jnp.sum(w.astype(f32) * g, axis=1) for w, g in zip((w_query, w_key, w_value), projections)
    ) / norm1_gain.astype(f32)

    normed_one = residual * inverse_one
    scaled = grad_hidden_one * gain_one
    grad_input = grad_middle + inverse_one * (
        scaled - normed_one * jnp.mean(scaled * normed_one, axis=-1, keepdims=True)
    )
    return (
        output[None],
        grad_input[None],
        grad_gain_one,
        gain_sums.sum(0),
        projections[0],
        projections[1],
        projections[2],
        dense[:, 3 * inner : 3 * inner + width],
        dense[:, :inner],
        dense[:, inner : 2 * inner],
        dense[:, 2 * inner : 3 * inner].T,
        expert_grads[0],
        expert_grads[1],
        expert_grads[2].astype(f32).transpose(0, 2, 1),
    )


def solution(mesh):
    by_token = P("dp", "ep", None)
    by_row = P(("dp", "ep"), None)
    in_specs = (
        (by_token,) * 5
        + (P(("dp", "ep")),) * 2
        + (by_row,) * 6
        + (P(None, ("dp", "ep")),)
        + (P("ep", None, None),) * 3
    )
    out_specs = (
        (by_token,) * 2
        + (P(("dp", "ep")),) * 2
        + (by_row,) * 6
        + (P(None, ("dp", "ep")), P("ep", "dp", None), P("ep", "dp", None), P("ep", None, "dp"))
    )
    return jax.shard_map(shards, mesh=mesh, in_specs=in_specs, out_specs=out_specs, check_vma=False)
```

```python
import math

import jax
import jax.numpy as jnp
from jax import lax
from jax.experimental import pallas as pl
from jax.experimental.pallas import tpu as pltpu
from jax.sharding import PartitionSpec as P

HEADS = 10
HEAD = 128
MAIN = 8
epsilon = 1e-06
negative = -1e30
bf16 = jnp.bfloat16
f32 = jnp.float32
VMEM_LIMIT = 64 * 1024 * 1024 - 128 * 1024


def dot(a, b):
    return jnp.dot(a, b, preferred_element_type=f32)


def dot_nt(a, b):
    return lax.dot_general(a, b, (((1,), (1,)), ((), ())), preferred_element_type=f32)


def dot_tn(a, b):
    return lax.dot_general(a, b, (((0,), (0,)), ((), ())), preferred_element_type=f32)


def tie(*values):
    return lax.optimization_barrier(values)


def after(value, *others):
    return lax.optimization_barrier((value, others))[0]


def cycle_of(size):
    if size == 16:
        return [0, 1, 2, 3, 7, 6, 5, 9, 10, 11, 15, 14, 13, 12, 8, 4]
    return list(range(0, size, 2)) + list(range(size - 1, 0, -2))


def spec(shape, index, single=False):
    if single:
        return pl.BlockSpec(shape, index, pipeline_mode=pl.Buffered(1))
    return pl.BlockSpec(shape, index)


class Ring:
    def __init__(self, size):
        self.size = size
        self.half = size // 2
        self.order = cycle_of(size)
        place = [0] * size
        for at, member in enumerate(self.order):
            place[member] = at
        self.forward = [(self.order[i], self.order[(i + 1) % size]) for i in range(size)]
        self.backward = [(self.order[i], self.order[(i - 1) % size]) for i in range(size)]
        table = [[self.order[(place[me] + offset) % size] for offset in range(size)] for me in range(size)]
        self.members = lax.dynamic_index_in_dim(jnp.array(table, jnp.int32), lax.axis_index("ep"), 0, keepdims=False)

    def member(self, offset):
        return self.members[offset % self.size]

    def step(self, up, down, number):
        if number == self.half:
            cut = up.shape[0] // 2
            up, down = up[:cut], down[cut:]
        return lax.ppermute(up, "ep", self.forward), lax.ppermute(down, "ep", self.backward)

    def gather(self, own, visit):
        up, down, arrived, done = own, own, (own,), None
        for step in range(1, self.half + 1):
            if done is not None:
                up, down, done = lax.optimization_barrier((up, down, done))
            up, down = self.step(up, down, step)
            done = visit(step - 1, arrived)
            arrived = (up, down)
        visit(self.half, arrived)

    def scatter_step(self, parts, came, number):
        cut = parts[0].shape[0] // 2
        away = self.half - number + 1
        if number == 1:
            up, down = parts[away][:cut], parts[away][cut:]
        else:
            ahead, behind = parts[away], parts[-away]
            up, down = came
            if number == 2:
                up = jnp.concatenate([(ahead[:cut].astype(f32) + up.astype(f32)).astype(bf16), ahead[cut:]], axis=0)
                down = jnp.concatenate([behind[:cut], (behind[cut:].astype(f32) + down.astype(f32)).astype(bf16)], axis=0)
            else:
                up = (ahead.astype(f32) + up.astype(f32)).astype(bf16)
                down = (behind.astype(f32) + down.astype(f32)).astype(bf16)
        return lax.ppermute(up, "ep", self.forward), lax.ppermute(down, "ep", self.backward)

    def scatter_end(self, parts, came):
        return parts[0].astype(f32) + came[0].astype(f32) + came[1].astype(f32)


def qkv_kernel(members_ref, tok_ref, gain_ref, w_ref, cos_ref, sin_ref, *rest):
    hid_ref, qkv_ref = rest[-2:]
    x = tok_ref[...].astype(f32)
    inverse = lax.rsqrt(jnp.mean(x * x, axis=-1, keepdims=True) + epsilon)
    hidden = (x * inverse * gain_ref[...]).astype(bf16)
    hid_ref[...] = hidden
    out = dot(hidden, w_ref[...])
    cosine, sine = cos_ref[...], sin_ref[...]
    for slot in range(6):
        u = out[:, slot * HEAD : (slot + 1) * HEAD]
        if slot % 3 != 2:
            u = u * cosine + pltpu.roll(u, HEAD // 2, 1) * sine
        qkv_ref[:, slot * HEAD : (slot + 1) * HEAD] = u.astype(bf16)


def qkv_piece(members, offset, shift, piece, tile, gain, w_cat, cosine, sine, buffers):
    rows, width = piece.shape
    length = cosine.shape[0]
    cols = w_cat.shape[1]
    aliased = () if buffers is None else tuple(buffers)
    n_in = 6
    at = lambda i, m: (2 * m[offset] + shift + i, 0)
    return pl.pallas_call(
        qkv_kernel,
        out_shape=(jax.ShapeDtypeStruct((length, width), bf16), jax.ShapeDtypeStruct((length, cols), bf16)),
        grid_spec=pltpu.PrefetchScalarGridSpec(
            num_scalar_prefetch=1,
            grid=(rows // tile,),
            in_specs=[
                pl.BlockSpec((tile, width), lambda i, b: (i, 0)),
                pl.BlockSpec((1, width), lambda i, b: (0, 0)),
                pl.BlockSpec((width, cols), lambda i, b: (0, 0)),
                pl.BlockSpec((tile, HEAD), at),
                pl.BlockSpec((tile, HEAD), at),
            ]
            + [pl.BlockSpec(memory_space=pl.ANY)] * len(aliased),
            out_specs=[
                pl.BlockSpec((tile, width), at),
                pl.BlockSpec((tile, cols), at),
            ],
        ),
        input_output_aliases={n_in + i: i for i in range(len(aliased))},
        compiler_params=pltpu.CompilerParams(vmem_limit_bytes=32 * 1024 * 1024),
        cost_estimate=pl.CostEstimate(
            flops=2 * rows * width * cols, bytes_accessed=4 * rows * width + 2 * (rows + width) * cols, transcendentals=0
        ),
        name="norm_project_rotate",
    )(members, piece, gain, w_cat, cosine, sine, *aliased)


def attention_forward(own, qkv, blocks, rows, main_rows, side_rows):
    scale = math.log2(math.e) / math.sqrt(HEAD)
    length = qkv.shape[0]
    tall = main_rows + side_rows

    def kernel(own_ref, qkv_ref, low_ref, att_ref, lse_ref):
        block = pl.program_id(0)

        def piece(col, offset, count):
            first = pl.multiple_of(block * rows + offset, 32)
            return qkv_ref[pl.ds(first, count), col : col + HEAD]

        offsets = (own_ref[0], own_ref[1])
        counts = (main_rows, side_rows)
        queries = [piece(3 * HEAD * i, offsets[i], counts[i]) for i in range(2)]

        def step(i, at, state, diagonal):
            best, total, acc = state
            first = pl.multiple_of(at * rows, rows)
            col = 3 * HEAD * i
            keys = qkv_ref[pl.ds(first, rows), col + HEAD : col + 2 * HEAD]
            values = qkv_ref[pl.ds(first, rows), col + 2 * HEAD : col + 3 * HEAD]
            scores = dot_nt(queries[i], keys) * scale
            if diagonal:
                q_at = lax.broadcasted_iota(jnp.int32, scores.shape, 0) + offsets[i]
                k_at = lax.broadcasted_iota(jnp.int32, scores.shape, 1)
                scores = jnp.where(q_at >= k_at, scores, negative)
            top = jnp.maximum(best, jnp.max(scores, axis=1, keepdims=True))
            weights = jnp.exp2(scores - top)
            factor = jnp.exp2(best - top)
            total = total * factor + jnp.sum(weights, axis=1, keepdims=True)
            acc = acc * factor + dot(weights.astype(bf16), values)
            return top, total, acc

        def both(at, states, diagonal=False):
            return tuple(step(i, at, states[i], diagonal) for i in range(2))

        start = tuple(
            (jnp.full((c, 1), negative, f32), jnp.zeros((c, 1), f32), jnp.zeros((c, HEAD), f32)) for c in counts
        )
        states = lax.fori_loop(0, block, both, start)
        states = both(block, states, True)
        at = 0
        for i in range(2):
            best, total, acc = states[i]
            attended = acc / total
            low_ref[0, at : at + counts[i]] = attended.astype(bf16)
            att_ref[0, at : at + counts[i]] = attended
            lse = jnp.broadcast_to(best + jnp.log2(total), (counts[i], HEAD))
            lse_ref[0, :, at : at + counts[i]] = jnp.transpose(lse)[0:8]
            at += counts[i]

    return pl.pallas_call(
        kernel,
        out_shape=(
            jax.ShapeDtypeStruct((blocks, tall, HEAD), bf16),
            jax.ShapeDtypeStruct((blocks, tall, HEAD), f32),
            jax.ShapeDtypeStruct((blocks, 8, tall), f32),
        ),
        grid_spec=pltpu.PrefetchScalarGridSpec(
            num_scalar_prefetch=1,
            grid=(blocks,),
            in_specs=[spec((length, qkv.shape[1]), lambda s, o: (0, 0), True)],
            out_specs=[
                pl.BlockSpec((1, tall, HEAD), lambda s, o: (s, 0, 0)),
                pl.BlockSpec((1, tall, HEAD), lambda s, o: (s, 0, 0)),
                pl.BlockSpec((1, 8, tall), lambda s, o: (s, 0, 0)),
            ],
        ),
        compiler_params=pltpu.CompilerParams(vmem_limit_bytes=48 * 1024 * 1024),
        cost_estimate=pl.CostEstimate(
            flops=4 * length * tall * blocks * HEAD // 2, bytes_accessed=16 * length * HEAD, transcendentals=length * tall * blocks // 2
        ),
        name="attention_forward",
    )(own, qkv)


def attention_backward(own, qkv, grads, attended, lse, cosine, sine, blocks, rows, count, slot, start, buffer=None):
    scale = 1.0 / math.sqrt(HEAD)
    scale_two = math.log2(math.e) * scale
    length = qkv.shape[0]
    tall = grads.shape[1]
    cols = 3 * HEAD
    here = slice(start, start + count)

    def kernel(own_ref, qkv_ref, grad_ref, att_ref, lse_ref, cos_ref, sin_ref, *rest):
        out_ref, key_sum, value_sum = rest[-3:]
        block = pl.program_id(0)
        offset = own_ref[slot]

        @pl.when(block == 0)
        def _():
            key_sum[...] = jnp.zeros_like(key_sum)
            value_sum[...] = jnp.zeros_like(value_sum)
            if count < rows:
                out_ref[:, :HEAD] = jnp.zeros((length, HEAD), bf16)

        mine = pl.multiple_of(block * rows + offset, 32)
        queries = qkv_ref[pl.ds(mine, count), :HEAD]
        grad = grad_ref[0, here]
        lse_row = lse_ref[0, 0:1, here]
        product = grad.astype(f32) * att_ref[0, here]
        delta = jnp.sum(jnp.transpose(product), axis=0, keepdims=True)

        def step(at, dq, diagonal=False):
            first = pl.multiple_of(at * rows, rows)
            keys = qkv_ref[pl.ds(first, rows), HEAD : 2 * HEAD]
            values = qkv_ref[pl.ds(first, rows), 2 * HEAD :]
            scores = dot_nt(keys, queries) * scale_two
            if diagonal:
                k_at = lax.broadcasted_iota(jnp.int32, scores.shape, 0)
                q_at = lax.broadcasted_iota(jnp.int32, scores.shape, 1) + offset
                scores = jnp.where(q_at >= k_at, scores, negative)
            probs = jnp.exp2(scores - lse_row)
            grad_probs = dot_nt(values, grad)
            grad_scores = (probs * (grad_probs - delta)).astype(bf16)
            value_sum[pl.ds(first, rows)] += dot(probs.astype(bf16), grad)
            key_sum[pl.ds(first, rows)] += dot(grad_scores, queries)
            return dq + dot_tn(grad_scores, keys)

        dq = step(block, lax.fori_loop(0, block, step, jnp.zeros((count, HEAD), f32)), True)

        def turn_back(value, first, size):
            cosine_part = cos_ref[pl.ds(first, size)]
            sine_part = sin_ref[pl.ds(first, size)]
            value = value * scale
            return (value * cosine_part - pltpu.roll(value, HEAD // 2, 1) * sine_part).astype(bf16)

        out_ref[pl.ds(mine, count), :HEAD] = turn_back(dq, mine, count)

        @pl.when(block == blocks - 1)
        def _():
            def finish(at, carry):
                first = pl.multiple_of(at * rows, rows)
                out_ref[pl.ds(first, rows), HEAD : 2 * HEAD] = turn_back(key_sum[pl.ds(first, rows)], first, rows)
                out_ref[pl.ds(first, rows), 2 * HEAD :] = value_sum[pl.ds(first, rows)].astype(bf16)
                return carry

            lax.fori_loop(0, blocks, finish, 0)

    aliased = () if buffer is None else (buffer,)
    return pl.pallas_call(
        kernel,
        out_shape=jax.ShapeDtypeStruct((length, 2 * cols), bf16),
        grid_spec=pltpu.PrefetchScalarGridSpec(
            num_scalar_prefetch=1,
            grid=(blocks,),
            in_specs=[
                spec((length, cols), lambda s, o: (0, slot), True),
                pl.BlockSpec((1, tall, HEAD), lambda s, o: (s, 0, 0)),
                pl.BlockSpec((1, tall, HEAD), lambda s, o: (s, 0, 0)),
                pl.BlockSpec((1, 8, tall), lambda s, o: (s, 0, 0)),
                spec((length, HEAD), lambda s, o: (0, 0), True),
                spec((length, HEAD), lambda s, o: (0, 0), True),
            ]
            + [pl.BlockSpec(memory_space=pl.ANY)] * len(aliased),
            out_specs=spec((length, cols), lambda s, o: (0, slot), True),
            scratch_shapes=[pltpu.VMEM((length, HEAD), f32)] * 2,
        ),
        input_output_aliases={7 + i: i for i in range(len(aliased))},
        compiler_params=pltpu.CompilerParams(vmem_limit_bytes=40 * 1024 * 1024),
        cost_estimate=pl.CostEstimate(
            flops=10 * length * count * blocks * HEAD // 2, bytes_accessed=20 * length * HEAD, transcendentals=length * count * blocks // 2
        ),
        name="attention_backward",
    )(own, qkv, grads, attended, lse, cosine, sine, *aliased)


def expert_call(members, offsets, hidden, grads, rank_row, rank_col, route, w_gate, w_up, w_down, capacity, first, total, buffers):
    count = len(hidden)
    rows, width = hidden[0].shape
    local, _, inner = w_gate.shape
    aliased = () if buffers is None else tuple(buffers)
    widths = (width, width, inner, inner, inner)

    def kernel(members_ref, *refs):
        h_refs, z_refs, row_refs, col_refs, gate_refs = (refs[i * count : (i + 1) * count] for i in range(5))
        wg_ref, wu_ref, wd_ref = refs[5 * count : 5 * count + 3]
        rest = refs[5 * count + 3 + len(aliased) :]
        outs_y, outs_x = rest[:count], rest[count : 2 * count]
        x_ref, dy_ref, a_ref, dg_ref, du_ref, keep_y, keep_x = rest[2 * count :]
        expert = pl.program_id(0)
        for p in range(count):
            slots = lax.broadcasted_iota(jnp.int32, (capacity, rows), 0).astype(f32)
            hit = slots == row_refs[p][0, expert]
            pick = jnp.where(hit, 1.0, 0.0).astype(bf16)
            gate = jnp.sum(jnp.where(hit, gate_refs[p][0, expert], 0.0), axis=1, keepdims=True)
            x = dot(pick, h_refs[p][...]).astype(bf16)
            dy = (dot(pick, z_refs[p][...]) * gate).astype(bf16)
            x_ref[0, p] = x
            dy_ref[0, p] = dy
            g = dot(x, wg_ref[0])
            u = dot(x, wu_ref[0])
            sigma = 1.0 / (1.0 + jnp.exp(-g))
            act = g * sigma
            a = (act * u).astype(bf16)
            a_ref[0, p] = a
            da = dot_nt(dy, wd_ref[0])
            du = (da * act).astype(bf16)
            dg = (da * u * sigma * (1.0 + g * (1.0 - sigma))).astype(bf16)
            du_ref[0, p] = du
            dg_ref[0, p] = dg
            y = dot(a, wd_ref[0]).astype(bf16)
            at = pl.multiple_of(expert * capacity, 16)
            keep_y[p, pl.ds(at, capacity)] = (y.astype(f32) * gate).astype(bf16)
            dx = dot_nt(dg, wg_ref[0]) + dot_nt(du, wu_ref[0])
            keep_x[p, pl.ds(at, capacity)] = dx.astype(bf16)

        @pl.when(expert == local - 1)
        def _():
            for p in range(count):
                slots = lax.broadcasted_iota(jnp.int32, (rows, capacity), 1).astype(f32)
                place = jnp.concatenate(
                    [jnp.where(slots == col_refs[p][0, e], 1.0, 0.0).astype(bf16) for e in range(local)], axis=1
                )
                outs_y[p][...] = dot(place, keep_y[p]).astype(bf16)
                outs_x[p][...] = dot(place, keep_x[p]).astype(bf16)

    piece = jax.ShapeDtypeStruct((rows, width), bf16)
    by_expert = lambda e, s: (e, 0, 0)
    slot = lambda e, s: (e, first // count, 0, 0)

    def of_source(shape):
        zeros = (0,) * (len(shape) - 1)
        return [pl.BlockSpec(shape, lambda e, s, p=p: (s[offsets[p]],) + zeros, pipeline_mode=pl.Buffered(1)) for p in range(count)]

    return pl.pallas_call(
        kernel,
        out_shape=[piece] * (2 * count) + [jax.ShapeDtypeStruct((local, total, capacity, w), bf16) for w in widths],
        grid_spec=pltpu.PrefetchScalarGridSpec(
            num_scalar_prefetch=1,
            grid=(local,),
            in_specs=[spec((rows, width), lambda e, s: (0, 0), True)] * (2 * count)
            + of_source((1, local, 1, rows))
            + of_source((1, local, rows, 1))
            + of_source((1, local, 1, rows))
            + [
                pl.BlockSpec((1, width, inner), by_expert),
                pl.BlockSpec((1, width, inner), by_expert),
                pl.BlockSpec((1, inner, width), by_expert),
            ]
            + [pl.BlockSpec(memory_space=pl.ANY)] * len(aliased),
            out_specs=[spec((rows, width), lambda e, s: (0, 0), True)] * (2 * count)
            + [pl.BlockSpec((1, count, capacity, w), slot) for w in widths],
            scratch_shapes=[pltpu.VMEM((count, local * capacity, width), bf16)] * 2,
        ),
        input_output_aliases={1 + 5 * count + 3 + i: 2 * count + i for i in range(len(aliased))},
        compiler_params=pltpu.CompilerParams(vmem_limit_bytes=VMEM_LIMIT),
        cost_estimate=pl.CostEstimate(
            flops=count * 2 * local * capacity * width * (6 * inner + 4 * rows),
            bytes_accessed=2 * local * (3 * width * inner + count * capacity * (2 * width + 3 * inner)) + count * 8 * rows * width,
            transcendentals=count * local * capacity * inner,
        ),
        name="experts",
    )(
        members,
        *hidden,
        *grads,
        *[rank_row] * count,
        *[rank_col] * count,
        *[route] * count,
        w_gate,
        w_up,
        w_down,
        *aliased,
    )


def shared_expert(hidden, grads, weights, inner):
    rows, width = hidden.shape
    tile = rows // 2

    def kernel(h_ref, z_ref, wg_ref, wu_ref, wd_ref, branch_ref, back_ref, act_ref, pre_ref):
        gate_pre = dot(h_ref[...], wg_ref[...])
        up_pre = dot(h_ref[...], wu_ref[...])
        grad_act = dot(z_ref[...], wd_ref[...])
        sigma = 1.0 / (1.0 + jnp.exp(-gate_pre))
        act = gate_pre * sigma
        low = (act * up_pre).astype(bf16)
        act_ref[...] = low
        grad_up = (grad_act * act).astype(bf16)
        grad_gate = (grad_act * up_pre * sigma * (1.0 + gate_pre * (1.0 - sigma))).astype(bf16)
        pre_ref[:, :inner] = grad_gate
        pre_ref[:, inner:] = grad_up
        branch_ref[...] = dot_nt(low, wd_ref[...])
        back_ref[...] = dot_nt(grad_gate, wg_ref[...]) + dot_nt(grad_up, wu_ref[...])

    by_row = lambda i: (i, 0)
    return pl.pallas_call(
        kernel,
        grid=(rows // tile,),
        out_shape=(
            jax.ShapeDtypeStruct((rows, width), f32),
            jax.ShapeDtypeStruct((rows, width), f32),
            jax.ShapeDtypeStruct((rows, inner), bf16),
            jax.ShapeDtypeStruct((rows, 2 * inner), bf16),
        ),
        in_specs=[pl.BlockSpec((tile, width), by_row)] * 2
        + [pl.BlockSpec((width, inner), lambda i, n=n: (0, n), pipeline_mode=pl.Buffered(1)) for n in range(3)],
        out_specs=[
            pl.BlockSpec((tile, width), by_row),
            pl.BlockSpec((tile, width), by_row),
            pl.BlockSpec((tile, inner), by_row),
            pl.BlockSpec((tile, 2 * inner), by_row),
        ],
        compiler_params=pltpu.CompilerParams(vmem_limit_bytes=40 * 1024 * 1024),
        cost_estimate=pl.CostEstimate(
            flops=12 * rows * width * inner, bytes_accessed=12 * rows * width + 6 * width * inner, transcendentals=rows * inner
        ),
        name="shared_expert",
    )(hidden, grads, weights, weights, weights)


def shards(
    tokens, cotangent, expert_ids, keep, gates, norm1_gain, norm2_gain, w_query, w_key, w_value, w_out,
    shared_gate, shared_up, shared_down, expert_gate, expert_up, expert_down,
):
    ep = lax.axis_size("ep")
    me = lax.axis_index("ep")
    ring = Ring(ep)
    half = ring.half
    token_rows = tokens[0]
    grad_low = cotangent[0]
    rows, width = token_rows.shape
    length = rows * ep
    local = expert_gate.shape[0]
    inner = expert_gate.shape[2]
    experts = local * ep
    shard = w_query.shape[0]
    copies = ep // MAIN
    sharers = MAIN // (HEADS - MAIN)
    main_rows = rows // copies
    side_rows = rows // (sharers * copies)
    tall = main_rows + side_rows
    capacity = min(rows, rows * 10 // experts)
    main_part = me % copies
    side_part = ((me // copies) % sharers) * copies + main_part
    own = jnp.stack([main_part * main_rows, side_part * side_rows]).astype(jnp.int32)

    gains = jnp.concatenate([norm1_gain[:, None], norm2_gain[:, None], jnp.zeros((shard, HEAD - 2), bf16)], axis=1)
    messages = []
    for member in range(ep):
        main_head = member // copies
        side_head = MAIN + main_head // sharers
        messages.append(
            jnp.concatenate(
                [
                    weight[:, head * HEAD : (head + 1) * HEAD]
                    for head in (main_head, side_head)
                    for weight in (w_query, w_key, w_value)
                ]
                + [gains],
                axis=1,
            )
        )
    head_rows = lax.all_to_all(jnp.stack(messages), "ep", 0, 0, tiled=True)

    chosen = expert_ids[0][:, :, None] == jnp.arange(experts, dtype=jnp.int32)[None, None, :]
    weight_here = gates[0] * keep[0].astype(f32)
    route = jnp.sum(jnp.where(chosen, weight_here[:, :, None], 0.0), axis=1)
    route = lax.all_to_all(route.T.reshape(ep, local, rows), "ep", 0, 0, tiled=True)
    used = route > 0.0
    before = (jnp.arange(rows)[:, None] < jnp.arange(rows)[None, :]).astype(bf16)
    rank = dot(used.astype(bf16).reshape(ep * local, rows), before).reshape(ep, local, rows)
    rank = jnp.where(used, rank, -1.0)

    freqs = jnp.exp(jnp.arange(HEAD // 2, dtype=f32) * (-2.0 * math.log(10000.0) / HEAD))
    turned = jnp.arange(length, dtype=jnp.int32).astype(f32)[:, None] * freqs[None, :]
    cosine, sine = jnp.cos(turned), jnp.sin(turned)
    cosine = jnp.concatenate([cosine, cosine], axis=1)
    sine = jnp.concatenate([-sine, sine], axis=1)

    tile = rows // 2
    arrivals, known = [], {}

    def project(steps):
        for step in steps:
            for i, part in enumerate(arrivals[step]):
                offset = 0 if step == 0 else (half if step == half else (-step, step)[i])
                known["buffers"] = qkv_piece(
                    ring.members, offset % ep, i if step == half else 0, part, tile, known["gains"][0], known["w_cat"],
                    cosine, sine, known.get("buffers"),
                )

    up, down = token_rows, token_rows
    arrivals.append((token_rows,))
    for step in range(1, half + 1):
        up, down = ring.step(up, down, step)
        if step == 1:
            head_rows, up, down = tie(head_rows, up, down)
            head_weights = lax.all_gather(head_rows.reshape(ep * shard, 7 * HEAD), "dp", axis=0, tiled=True)
            gain_rows = head_weights[:, 6 * HEAD : 6 * HEAD + 2].astype(f32).T
            gain_one, gain_two = gain_rows[0:1], gain_rows[1:2]
            w_cat = head_weights[:, : 6 * HEAD]
            known["gains"], known["w_cat"] = (gain_one, gain_two), w_cat
        if step == 2:
            route, rank, up, down = tie(route, rank, up, down)
        if step == half - 1:
            project(range(half - 1))
            packed = jnp.concatenate([w_out, shared_gate, shared_up, shared_down.T], axis=1)
            up, down, packed, known["buffers"] = tie(up, down, packed, known["buffers"])
            packed = lax.all_gather(packed, "ep", axis=0, tiled=True)
        arrivals.append((up, down))
    project([half - 1, half])
    hidden_all, qkv = known["buffers"]

    grad_pieces = {0: (grad_low,)}
    grad_low, qkv = tie(grad_low, qkv)
    grad_pieces[1] = ring.step(grad_low, grad_low, 1)

    low, attended, lse = attention_forward(own, qkv, ep, rows, main_rows, side_rows)
    low, grad_pieces[1], packed = tie(low, grad_pieces[1], packed)
    full_out = lax.all_gather(packed[:, :width], "dp", axis=0, tiled=True)
    grad_pieces[2] = ring.step(*grad_pieces[1], 2)
    heads_in = lax.all_to_all(low, "ep", 0, 0, tiled=True)
    rank_row, rank_col, route_row = rank[:, :, None, :], rank[:, :, :, None], route[:, :, None, :]
    heads_in, rank_col = tie(heads_in, rank_col)
    main_in = heads_in[:, :main_rows].reshape(MAIN, rows, HEAD)
    side_in = heads_in[:, main_rows:].reshape(HEADS - MAIN, rows, HEAD)
    attended_low = jnp.concatenate([main_in, side_in], axis=0).transpose(1, 0, 2).reshape(rows, width)

    residual = token_rows.astype(f32)
    middle = residual + dot(attended_low, full_out)
    inverse_two = lax.rsqrt(jnp.mean(middle * middle, axis=-1, keepdims=True) + epsilon)
    normed_two = middle * inverse_two
    hidden_two = (normed_two * gain_two).astype(bf16)

    hidden_two, grad_pieces[2], packed = tie(hidden_two, grad_pieces[2], packed)
    packed = lax.all_gather(packed[:, width:], "dp", axis=0, tiled=True)
    part_y, part_x, buffers = {}, {}, [None]

    def run_experts(step, arrived):
        grads = grad_pieces[step]
        if step == half:
            group, first = (half,), ep - 1
        elif step == 0:
            group, first = (0,), ep - 2
        else:
            group, first = (-step, step), 2 * (step - 1)
        outs = expert_call(
            ring.members,
            [offset % ep for offset in group],
            arrived,
            grads,
            rank_row,
            rank_col,
            route_row,
            expert_gate,
            expert_up,
            expert_down,
            capacity,
            first,
            ep,
            buffers[0],
        )
        for i, offset in enumerate(group):
            part_y[offset] = outs[i]
            part_x[offset] = outs[len(group) + i]
        buffers[0] = outs[2 * len(group) :]
        return outs[len(group)]

    def run_shared(hidden, grads):
        branch, back, act, grad_pre = shared_expert(hidden, grads, packed, inner)
        return branch, back, dot_tn(hidden, grad_pre).astype(bf16), dot_tn(grads, act).astype(bf16)

    up, down, arrived = hidden_two, hidden_two, (hidden_two,)
    for step in range(1, half + 1):
        if step < half:
            up, down = ring.step(up, down, step)
            if step >= 4:
                grad_pieces[step] = ring.step(*grad_pieces[step - 1], step)
        else:
            up = lax.ppermute(up, "ep", ring.forward)
            grad_pieces[step] = (lax.ppermute(grad_pieces[step - 1][1], "ep", ring.backward),)
        done = run_experts(step - 1, arrived)
        up, down, done, grad_pieces[step] = tie(up, down, done, grad_pieces[step])
        if step == 2:
            hidden_two, grad_low, done = tie(hidden_two, grad_low, done)
            shared = run_shared(hidden_two, grad_low)
            arrived = (up, down)
            if half > 3:
                grad_pieces[3] = ring.step(*grad_pieces[2], 3)
                grad_pieces[3], done, shared, arrived = tie(grad_pieces[3], done, shared, arrived)
            else:
                done, shared, arrived = tie(done, shared, arrived)
            dense = [lax.psum_scatter(item, "dp", scatter_dimension=0, tiled=True) for item in shared[2:]]
        else:
            arrived = (up, down) if step < half else (up,)
        if step == half:
            done, dense = tie(done, dense)
        part_x[(0 if step == 1 else 1 - step)] = done
    run_experts(half, arrived)
    shared_branch, grad_shared = shared[:2]
    saved_x, saved_dy, saved_a, saved_dg, saved_du = [
        item.reshape(local, ep * capacity, item.shape[-1]) for item in buffers[0]
    ]

    def by_rows(left, right):
        return jnp.einsum("ecd,ecf->edf", left, right, preferred_element_type=f32).astype(bf16)

    came, expert_grads = None, []
    for step in range(1, half + 1):
        came = ring.scatter_step(part_x, came, step)
        if step <= 3:
            left, right = ((saved_x, saved_dg), (saved_x, saved_du), (saved_dy, saved_a))[step - 1]
            item = by_rows(left, right)
            came, item = tie(came, item)
            if step < 3:
                item = lax.psum_scatter(item, "dp", scatter_dimension=1, tiled=True)
            expert_grads.append(item)
    came, expert_grads[0] = tie(came, expert_grads[0])
    grad_routed = ring.scatter_end(part_x, came)
    grad_hidden_two = grad_shared + grad_routed
    grad_gain_two = jnp.sum(grad_hidden_two * normed_two, axis=0)
    scaled = grad_hidden_two * gain_two
    grad_out = grad_low.astype(f32)
    grad_middle = grad_out + inverse_two * (
        scaled - normed_two * jnp.mean(scaled * normed_two, axis=-1, keepdims=True)
    )
    grad_branch = grad_middle.astype(bf16)
    grad_attended = dot_nt(grad_branch, full_out).astype(bf16)

    by_head = grad_attended.reshape(rows, HEADS, HEAD).transpose(1, 0, 2)
    heads_out = jnp.concatenate(
        [by_head[:MAIN].reshape(ep, main_rows, HEAD), by_head[MAIN:].reshape(ep, side_rows, HEAD)], axis=1
    )
    part_y[half], grad_routed = tie(part_y[half], grad_routed)
    came_y = ring.scatter_step(part_y, None, 1)
    heads_out, attended_low, grad_branch, grad_gain_two = tie(heads_out, attended_low, grad_branch, grad_gain_two)
    head_grads = lax.all_to_all(heads_out, "ep", 0, 0, tiled=True)
    grad_full_out = dot_tn(attended_low, grad_branch).astype(bf16)

    gain_high = grad_gain_two.astype(bf16)
    gain_rest = (grad_gain_two - gain_high.astype(f32)).astype(bf16)
    gain_columns = dot_tn(jnp.stack([gain_high, gain_rest]), jnp.eye(2, HEAD, dtype=bf16))
    head_grads, came_y, grad_full_out, expert_grads[1] = tie(head_grads, came_y, grad_full_out, expert_grads[1])
    dense.append(lax.psum_scatter(grad_full_out, "dp", scatter_dimension=0, tiled=True))
    for step in range(2, half - 1):
        came_y = ring.scatter_step(part_y, came_y, step)
    grad_side = attention_backward(
        own, qkv, head_grads, attended, lse, cosine, sine, ep, rows, side_rows, 1, main_rows
    )
    grad_side, came_y, qkv, dense = tie(grad_side, came_y, qkv, dense)
    dense = lax.psum_scatter(jnp.concatenate(dense, axis=1), "ep", scatter_dimension=0, tiled=True).astype(f32)
    came_y = ring.scatter_step(part_y, came_y, half - 1)
    grad_main = attention_backward(
        own, qkv, head_grads, attended, lse, cosine, sine, ep, rows, main_rows, 0, 0, grad_side
    )
    grad_qkv, came_y, expert_grads[:2] = tie(grad_main, came_y, expert_grads[:2])
    came_y = ring.scatter_step(part_y, came_y, half)

    part_h = {}
    for offset in range(-half + 1, half + 1):
        block = lax.dynamic_slice_in_dim(grad_qkv, ring.member(offset) * rows, rows, 0)
        part_h[offset] = dot_nt(block, w_cat).astype(bf16)
    came = None
    inverse_one = lax.rsqrt(jnp.mean(residual * residual, axis=-1, keepdims=True) + epsilon)
    for step in range(1, half + 1):
        came = ring.scatter_step(part_h, came, step)
        if step == 1:
            next_parts = [part_h[offset] for offset in (half - 1, 1 - half)]
            came, next_parts, hidden_all = tie(came, next_parts, hidden_all)
            part_h[half - 1], part_h[1 - half] = next_parts
            head_sums = jnp.concatenate([dot_tn(hidden_all, grad_qkv), gain_columns], axis=1).astype(bf16)
            came_y, head_sums = tie(came_y, head_sums)
            head_sums = lax.psum_scatter(head_sums, "dp", scatter_dimension=0, tiled=True)
        if step == 2:
            early = [item.astype(f32) for item in expert_grads[:2]]
            came, came_y, part_h, expert_grads[:2], inverse_one = tie(came, came_y, part_h, early, inverse_one)
            output = (middle + shared_branch + ring.scatter_end(part_y, came_y)).astype(bf16)
        if step == 3:
            came, head_sums, dense, last, output = tie(came, head_sums, dense, expert_grads[2], output)
            head_sums = lax.all_to_all(head_sums.reshape(ep, shard, 7 * HEAD), "ep", 0, 0, tiled=True)
            expert_grads[2] = lax.psum_scatter(last, "dp", scatter_dimension=1, tiled=True)
    head_sums = head_sums.astype(f32)
    grad_hidden_one = ring.scatter_end(part_h, came)
    main_sums = head_sums[:, :, : 3 * HEAD].reshape(MAIN, copies, shard, 3, HEAD).sum(1)
    gain_sums = head_sums[:, :, 6 * HEAD] + head_sums[:, :, 6 * HEAD + 1]
    side_sums = head_sums[:, :, 3 * HEAD : 6 * HEAD].reshape(HEADS - MAIN, sharers * copies, shard, 3, HEAD).sum(1)
    head_sums = jnp.concatenate([main_sums, side_sums], axis=0)
    projections = [head_sums[:, :, i].transpose(1, 0, 2).reshape(shard, width) for i in range(3)]
    grad_gain_one = sum(
        jnp.sum(w.astype(f32) * g, axis=1) for w, g in zip((w_query, w_key, w_value), projections)
    ) / norm1_gain.astype(f32)

    normed_one = residual * inverse_one
    scaled = grad_hidden_one * gain_one
    grad_input = grad_middle + inverse_one * (
        scaled - normed_one * jnp.mean(scaled * normed_one, axis=-1, keepdims=True)
    )
    return (
        output[None],
        grad_input[None],
        grad_gain_one,
        gain_sums.sum(0),
        projections[0],
        projections[1],
        projections[2],
        dense[:, 3 * inner : 3 * inner + width],
        dense[:, :inner],
        dense[:, inner : 2 * inner],
        dense[:, 2 * inner : 3 * inner].T,
        expert_grads[0],
        expert_grads[1],
        expert_grads[2].astype(f32).transpose(0, 2, 1),
    )


def solution(mesh):
    by_token = P("dp", "ep", None)
    by_row = P(("dp", "ep"), None)
    in_specs = (
        (by_token,) * 5
        + (P(("dp", "ep")),) * 2
        + (by_row,) * 6
        + (P(None, ("dp", "ep")),)
        + (P("ep", None, None),) * 3
    )
    out_specs = (
        (by_token,) * 2
        + (P(("dp", "ep")),) * 2
        + (by_row,) * 6
        + (P(None, ("dp", "ep")), P("ep", "dp", None), P("ep", "dp", None), P("ep", None, "dp"))
    )
    return jax.shard_map(shards, mesh=mesh, in_specs=in_specs, out_specs=out_specs, check_vma=False)
```
